256 devices in a mesh: rep: 16 (over y_lo, x, core), exp: 16 (over y_hi, z).
Axes of the slice: x: 4, y: 4 (y_hi: 2, y_lo: 2; y = y_hi * 2 + y_lo), z: 8, core: 2. Of those that a mesh axis runs over, the one named last changes fastest.
Arguments:
- grad_out: bfloat16 [32768, 3584], P(('rep', 'exp')), may hold values from -6 to 6
- routes: int32 [32768, 4], P(('rep', 'exp')), may hold values from 0 to 15, as said below
- affinity: float32 [32768, 4], P(('rep', 'exp')), may hold values from 0.02 to 0.98
- saved_hidden: bfloat16 [16, 16, 16, 60, 1024], P('rep', 'exp'), may hold values from -0.29882812 to 0.29882812
- down_proj: bfloat16 [1024, 16, 3584], P('rep', 'exp'), may hold values from -0.1875 to 0.1875
Outputs:
- affinity_grad: float32 [32768, 4], P(('rep', 'exp'))
- hidden_grad: bfloat16 [16, 16, 16, 60, 1024], P('rep', 'exp')
- down_grad: float32 [1024, 16, 3584], P('rep', 'exp')
The draws below stay inside these ranges and needn't reach their ends.
Inputs may be any that keep to these rules, and one draw needn't show every extreme that they name: `routes`: each row names 4 different experts. Among the tokens of one device no expert is named more than 60 times; in every replica group one expert is named exactly 60 times by the tokens of each device of the group.
All inputs are finite; a program needn't handle non-finite values.
Results may differ from the reference program's by a relative error of at most 0.02.
Values may be sent and summed in bfloat16 or wider, within the bound.
A program may use at most 128 MiB of HBM per device.

```python
import math
from functools import partial
import jax
import jax.numpy as jnp
from jax import lax

D = 3584
H = 1024
EXPERTS = 16
TOPK = 4
TOK_DEV = 128
MOST = 60
TOKENS = 32768
N_REP = 16
N_EXP = 16


def device_routes(dev_key, busy_expert):
    key_shuffle, key_space, key_open, key_other, key_rotate = jax.random.split(dev_key, 5)
    shuffle = jax.random.permutation(key_shuffle, TOK_DEV)
    leading = (jnp.arange(TOK_DEV) < MOST).astype(jnp.int32)
    is_busy = jnp.zeros((TOK_DEV,), jnp.int32).at[shuffle].set(leading)
    needed = TOPK - is_busy
    spacing = jax.random.randint(key_space, (TOK_DEV,), 0, 3)
    advance = needed + spacing
    opening = jnp.cumsum(advance) - advance + jax.random.randint(key_open, (), 0, EXPERTS - 1)
    others = jax.random.permutation(key_other, EXPERTS - 1).astype(jnp.int32)
    others = others + (others >= busy_expert).astype(jnp.int32)
    window = (opening[:, None] + jnp.arange(TOPK)[None, :]) % (EXPERTS - 1)
    chosen = others[window]
    with_busy = jnp.concatenate([jnp.broadcast_to(busy_expert, (TOK_DEV, 1)).astype(jnp.int32), chosen[:, :TOPK - 1]], axis=1)
    merged = jnp.where(is_busy[:, None] > 0, with_busy, chosen)
    rotation = jax.random.randint(key_rotate, (TOK_DEV, 1), 0, TOPK)
    column = (jnp.arange(TOPK)[None, :] + rotation) % TOPK
    return jnp.take_along_axis(merged, column, axis=1)


def draw_routes(key, part):
    key_busy, key_rest = jax.random.split(key)
    busiest = jax.random.randint(key_busy, (N_REP,), 0, EXPERTS).astype(jnp.int32)
    busy_devices = jnp.repeat(busiest, N_EXP)
    device_keys = jax.random.split(key_rest, N_REP * N_EXP)
    drawn = jax.vmap(device_routes)(device_keys, busy_devices)
    return drawn.reshape(TOKENS, TOPK).astype(jnp.int32)


def with_spikes(entries, own_key, source, target, blocks, factor):
    def block_of(axis_at):
        return (jnp.arange(entries.shape[axis_at]) // (entries.shape[axis_at] // blocks)).reshape((-1,) + (1,) * (entries.ndim - 1 - axis_at))

    first = jax.random.permutation(own_key, blocks)[block_of(target)]
    other_side = (block_of(target) + blocks // 2) % blocks
    return jnp.where((block_of(source) == first) | (block_of(source) == other_side), factor * entries, entries)


def block_levels(key, shape, cuts, least, high):
    level = 1.0
    for position, blocks in cuts:
        heights = jax.random.uniform(jax.random.fold_in(jax.random.fold_in(key, 6), position), (blocks,), jnp.float32, least / len(cuts), high / len(cuts))
        level = level * jnp.repeat(jnp.exp(heights), shape[position] // blocks).reshape((-1,) + (1,) * (len(shape) - 1 - position))
    return level


def bell_draw(own_key, extent, width, limit, cuts=(), held_as=jnp.bfloat16):
    loudness = block_levels(own_key, extent, cuts, -0.22, 0.18) if cuts else 1.0
    result = jax.random.normal(own_key, extent, jnp.float32) * width * loudness
    return jnp.minimum(jnp.maximum(result, -limit), limit).astype(held_as)


def bell_draw_with(rng, extent, spread, bound, shards, heavy, kind=jnp.bfloat16):
    values = spread * jax.random.normal(rng, extent, jnp.float32)
    if shards:
        values = values * block_levels(rng, extent, shards, -0.22, 0.18)
    return jnp.clip(with_spikes(values, jax.random.fold_in(rng, 3), *heavy), -bound, bound).astype(kind)


def setup_inputs(seed: int = 0) -> dict:
    splits = jax.random.split(jax.random.key(seed), 6)
    grad_out = bell_draw(splits[0], (TOKENS, D), 1.0, 6.0, ((0, 256),))
    routes = draw_routes(jax.random.fold_in(splits[5], 71), 0)
    affinity = jnp.clip(jnp.exp(math.log(0.98) - 3.89182034 * jax.random.uniform(splits[2], (TOKENS, TOPK), jnp.float32) ** block_levels(splits[2], (TOKENS, TOPK), ((0, 256),), -0.2, 0.2)), 0.02, 0.98)
    saved_hidden = bell_draw_with(splits[3], (N_REP, EXPERTS, N_EXP, MOST, H), 0.05, 0.29882812, ((0, 16), (1, 16)), (0, 4, 16, 2.0))
    down_proj = bell_draw(splits[4], (H, EXPERTS, D), H ** -0.5, 0.1875, ((0, 16), (1, 16)))
    return {"grad_out": grad_out, "routes": routes, "affinity": affinity, "saved_hidden": saved_hidden, "down_proj": down_proj}


ROUTE_SCALE = 2.5


def pack_routes(grad_rows, route_ids, route_weight, expert_count, most):
    expert_ids = jnp.arange(expert_count, dtype=jnp.int32)
    naming = jnp.sum((route_ids[:, :, None] == expert_ids[None, None, :]).astype(jnp.int32), axis=1)
    before = jnp.cumsum(naming, axis=0) - naming
    slot_ids = jnp.take_along_axis(before, route_ids, axis=1).astype(jnp.int32)
    placed = (route_ids * most + slot_ids).reshape(-1).astype(jnp.int32)
    token_ids = jnp.repeat(jnp.arange(grad_rows.shape[0], dtype=jnp.int32), route_ids.shape[1])
    source = jnp.zeros((expert_count * most,), jnp.int32).at[placed].set(token_ids)
    filled = jnp.zeros((expert_count * most,), jnp.int32).at[placed].set(1)
    weights = jnp.zeros((expert_count * most,), route_weight.dtype).at[placed].set(route_weight.reshape(-1))
    fetched = jnp.take(grad_rows, source, axis=0)
    packed = jnp.where(filled[:, None] > 0, fetched, jnp.zeros_like(fetched))
    return packed.reshape(expert_count, most, grad_rows.shape[1]), weights.reshape(expert_count, most), placed


def reference(grad_out, routes, affinity, saved_hidden, down_proj):
    grad_grid = grad_out.reshape(N_REP, N_EXP, TOK_DEV, D)
    route_grid = routes.reshape(N_REP, N_EXP, TOK_DEV, TOPK)
    affinity_grid = affinity.reshape(N_REP, N_EXP, TOK_DEV, TOPK)
    weights_wide = down_proj.astype(jnp.float32)
    packer = jax.vmap(partial(pack_routes, expert_count=EXPERTS, most=MOST))

    def per_group(running, inputs):
        grad_group, route_group, affinity_group, hidden_group = inputs
        totals = jnp.sum(affinity_group, axis=-1, keepdims=True)
        shares = affinity_group / totals
        route_weight = (ROUTE_SCALE * shares).astype(jnp.bfloat16)
        packed, packed_weight, placed = packer(grad_group, route_group, route_weight)
        received = jnp.transpose(packed, (1, 0, 2, 3)).reshape(EXPERTS, N_EXP * MOST, D).astype(jnp.float32)
        row_scale = jnp.transpose(packed_weight, (1, 0, 2)).reshape(EXPERTS, N_EXP * MOST).astype(jnp.float32)
        hidden = hidden_group.reshape(EXPERTS, N_EXP * MOST, H).astype(jnp.float32)
        projected = jnp.einsum('erd,hed->erh', received, weights_wide)
        hidden_grad = (row_scale[:, :, None] * projected).astype(jnp.bfloat16)
        combine_grad = ROUTE_SCALE * jnp.sum(hidden * projected, axis=-1)
        scaled = lax.optimization_barrier((row_scale[:, :, None] * received).astype(jnp.bfloat16)).astype(jnp.float32)
        partial_grad = jnp.einsum('erh,erd->hed', hidden, scaled)
        partial_grad = lax.optimization_barrier(partial_grad.astype(jnp.bfloat16)).astype(jnp.float32)
        running = running + partial_grad
        returned = jnp.transpose(combine_grad.reshape(EXPERTS, N_EXP, MOST), (1, 0, 2)).reshape(N_EXP, EXPERTS * MOST)
        route_grad = jnp.take_along_axis(returned, placed, axis=1).reshape(N_EXP, TOK_DEV, TOPK)
        affinity_grad = (route_grad - jnp.sum(route_grad * shares, axis=-1, keepdims=True)) / totals
        return running, (affinity_grad, hidden_grad.reshape(EXPERTS, N_EXP, MOST, H))

    zero_grad = jnp.zeros((H, EXPERTS, D), jnp.float32)
    down_grad, outputs = lax.scan(per_group, zero_grad, (grad_grid, route_grid, affinity_grid, saved_hidden))
    affinity_grad, hidden_grad = outputs
    return affinity_grad.reshape(TOKENS, TOPK), hidden_grad, down_grad
```

```python
import jax
import jax.numpy as jnp
from jax import lax
from jax.sharding import Mesh
from jax.sharding import PartitionSpec as P

ROUTE_SCALE = 2.5
TOKENS_SPEC = ("rep", "yh", "z")


def slots_of(routes, expert_count):
    expert_ids = jnp.arange(expert_count, dtype=jnp.int32)
    naming = jnp.sum((routes[..., None] == expert_ids).astype(jnp.int32), axis=2)
    before = jnp.cumsum(naming, axis=1) - naming
    return jnp.take_along_axis(before, routes, axis=2)


def selection(routes, slots, route_weight, expert, most):
    names = routes == expert
    position = jnp.sum(jnp.where(names, slots + 1, 0), axis=2) - 1
    weight = jnp.sum(jnp.where(names, route_weight.astype(jnp.float32), 0.0), axis=2)
    picks = position[:, None, :] == jnp.arange(most, dtype=jnp.int32)[None, :, None]
    packed_weight = jnp.sum(jnp.where(picks, weight[:, None, :], 0.0), axis=2)
    return picks.astype(jnp.bfloat16), packed_weight


def on_device(grad_out, routes, affinity, saved_hidden, down_proj):
    n_yh = lax.axis_size("yh")
    n_z = lax.axis_size("z")
    exp_devices = n_yh * n_z
    local_experts = down_proj.shape[1]
    expert_count = exp_devices * local_experts
    most = saved_hidden.shape[3]
    width = grad_out.shape[1]
    hidden_units = saved_hidden.shape[4]
    tok = grad_out.shape[0]
    yh = lax.axis_index("yh")
    z = lax.axis_index("z")
    me = yh * n_z + z
    partner_yh = (yh + 1) % n_yh
    mine = me
    partner = partner_yh * n_z + z

    all_routes = lax.all_gather(routes, ("yh", "z"), axis=0, tiled=False)
    all_affinity = lax.all_gather(affinity, ("yh", "z"), axis=0, tiled=False)
    totals_all = jnp.sum(all_affinity, axis=-1, keepdims=True)
    shares_all = all_affinity / totals_all
    weight_all = (ROUTE_SCALE * shares_all).astype(jnp.bfloat16)
    slots_all = slots_of(all_routes, expert_count)

    plane = lambda x, p: lax.dynamic_slice_in_dim(x, p * n_z, n_z, axis=0)
    pick_mine, weight_mine = selection(
        plane(all_routes, yh), plane(slots_all, yh), plane(weight_all, yh), mine, most
    )
    pick_partner, _ = selection(
        plane(all_routes, yh), plane(slots_all, yh), plane(weight_all, yh), partner, most
    )
    pick_far, weight_far = selection(
        plane(all_routes, partner_yh),
        plane(slots_all, partner_yh),
        plane(weight_all, partner_yh),
        mine,
        most,
    )
    del pick_far

    gathered = lax.all_gather(grad_out, "z", axis=0, tiled=False)
    near_rows = jnp.einsum(
        "sjt,std->sjd", pick_mine, gathered, preferred_element_type=jnp.float32
    ).astype(jnp.bfloat16)
    outgoing = jnp.einsum(
        "sjt,std->sjd", pick_partner, gathered, preferred_element_type=jnp.float32
    ).astype(jnp.bfloat16)
    far_rows = lax.ppermute(
        outgoing, "yh", perm=[(i, (i + 1) % n_yh) for i in range(n_yh)]
    )

    hidden = saved_hidden.reshape(exp_devices, most, hidden_units)
    near_hidden = plane(hidden, yh).reshape(n_z * most, hidden_units)
    far_hidden = plane(hidden, partner_yh).reshape(n_z * most, hidden_units)
    gathered_w = lax.all_gather(down_proj, "rep", axis=0, tiled=True).reshape(
        hidden_units, width
    )

    def expert_side(rows, row_weight, hid):
        rows = rows.reshape(n_z * most, width)
        scale = row_weight.reshape(n_z * most, 1)
        projected = jnp.einsum(
            "rd,hd->rh", rows, gathered_w, preferred_element_type=jnp.float32
        )
        hidden_grad = (scale * projected).astype(jnp.bfloat16)
        combine = ROUTE_SCALE * jnp.sum(hid.astype(jnp.float32) * projected, axis=-1)
        scaled = (scale * rows.astype(jnp.float32)).astype(jnp.bfloat16)
        term = jnp.einsum("rh,rd->hd", hid, scaled, preferred_element_type=jnp.float32)
        return hidden_grad, combine, term

    near_grad, near_combine, near_term = expert_side(near_rows, weight_mine, near_hidden)
    far_grad, far_combine, far_term = expert_side(far_rows, weight_far, far_hidden)
    grad_term = near_term + far_term
    down_grad = lax.psum_scatter(
        grad_term.astype(jnp.bfloat16), "rep", scatter_dimension=0, tiled=True
    ).astype(jnp.float32)

    first = yh == 0
    hidden_grad = jnp.where(
        first,
        jnp.concatenate([near_grad, far_grad], axis=0),
        jnp.concatenate([far_grad, near_grad], axis=0),
    )
    combine_grad = jnp.where(
        first,
        jnp.concatenate([near_combine, far_combine], axis=0),
        jnp.concatenate([far_combine, near_combine], axis=0),
    ).reshape(exp_devices, most)
    returned = lax.all_to_all(
        combine_grad, ("yh", "z"), split_axis=0, concat_axis=0, tiled=True
    )
    my_routes = routes
    my_slots = lax.dynamic_index_in_dim(slots_all, me, axis=0, keepdims=False)
    placed = my_routes * most + my_slots
    route_grad = jnp.take(returned.reshape(-1), placed.reshape(-1)).reshape(routes.shape)
    totals = jnp.sum(affinity, axis=-1, keepdims=True)
    shares = affinity / totals
    affinity_grad = (route_grad - jnp.sum(route_grad * shares, axis=-1, keepdims=True)) / totals
    return (
        affinity_grad,
        hidden_grad.reshape(saved_hidden.shape),
        down_grad.reshape(down_proj.shape),
    )


def solution(mesh):
    n_exp = mesh.shape["exp"]
    n_yh = 2
    split = Mesh(
        mesh.devices.reshape(mesh.shape["rep"], n_yh, n_exp // n_yh),
        ("rep", "yh", "z"),
    )
    return jax.shard_map(
        on_device,
        mesh=split,
        in_specs=(
            P(TOKENS_SPEC, None),
            P(TOKENS_SPEC, None),
            P(TOKENS_SPEC, None),
            P("rep", ("yh", "z"), None, None, None),
            P("rep", ("yh", "z"), None),
        ),
        out_specs=(
            P(TOKENS_SPEC, None),
            P("rep", ("yh", "z"), None, None, None),
            P("rep", ("yh", "z"), None),
        ),
        check_vma=False,
    )
```

```python
import jax
import jax.numpy as jnp
from jax import lax
from jax.sharding import Mesh
from jax.sharding import PartitionSpec as P

ROUTE_SCALE = 2.5
TOKENS_SPEC = ("rep", "yh", "z")
META = 128


def local_slots(routes, expert_count):
    tok = routes.shape[0]
    expert_ids = jnp.arange(expert_count, dtype=jnp.int32)
    hits = routes[:, :, None] == expert_ids
    naming = jnp.sum(hits.astype(jnp.float32), axis=1)
    earlier = (
        jnp.arange(tok, dtype=jnp.int32)[None, :] < jnp.arange(tok, dtype=jnp.int32)[:, None]
    ).astype(jnp.bfloat16)
    before = jnp.dot(earlier, naming.astype(jnp.bfloat16), preferred_element_type=jnp.float32)
    return jnp.sum(jnp.where(hits, before[:, None, :], 0.0), axis=2)


def selection(route_f, slot_f, weight_f, expert, most):
    names = route_f == expert.astype(jnp.float32)
    position = jnp.sum(jnp.where(names, slot_f + 1.0, 0.0), axis=2) - 1.0
    weight = jnp.sum(jnp.where(names, weight_f, 0.0), axis=2)
    picks = position[:, None, :] == jnp.arange(most, dtype=jnp.float32)[None, :, None]
    packed_weight = jnp.sum(jnp.where(picks, weight[:, None, :], 0.0), axis=2)
    return picks.astype(jnp.bfloat16), packed_weight


def on_device(grad_out, routes, affinity, saved_hidden, down_proj):
    n_yh = lax.axis_size("yh")
    n_z = lax.axis_size("z")
    exp_devices = n_yh * n_z
    local_experts = down_proj.shape[1]
    expert_count = exp_devices * local_experts
    most = saved_hidden.shape[3]
    width = grad_out.shape[1]
    hidden_units = saved_hidden.shape[4]
    topk = routes.shape[1]
    yh = lax.axis_index("yh")
    z = lax.axis_index("z")
    partner_yh = (yh + 1) % n_yh
    mine = yh * n_z + z
    partner = partner_yh * n_z + z

    totals = jnp.sum(affinity, axis=-1, keepdims=True)
    shares = affinity / totals
    route_weight = (ROUTE_SCALE * shares).astype(jnp.bfloat16)
    slots = local_slots(routes, expert_count)
    meta = jnp.concatenate(
        [
            routes.astype(jnp.bfloat16),
            slots.astype(jnp.bfloat16),
            route_weight,
            jnp.zeros((routes.shape[0], META - 3 * topk), jnp.bfloat16),
        ],
        axis=1,
    )
    carried = jnp.concatenate([grad_out, meta], axis=1)
    gathered = lax.all_gather(carried, "z", axis=0, tiled=False)
    meta_all = gathered[:, :, width : width + 3 * topk].astype(jnp.float32)
    route_f = meta_all[:, :, 0:topk]
    slot_f = meta_all[:, :, topk : 2 * topk]
    weight_f = meta_all[:, :, 2 * topk : 3 * topk]

    pick_mine, weight_mine = selection(route_f, slot_f, weight_f, mine, most)
    pick_partner, weight_partner = selection(route_f, slot_f, weight_f, partner, most)
    near_rows = jnp.einsum(
        "sjt,std->sjd", pick_mine, gathered, preferred_element_type=jnp.float32
    ).astype(jnp.bfloat16)[:, :, :width]
    outgoing = jnp.einsum(
        "sjt,std->sjd", pick_partner, gathered, preferred_element_type=jnp.float32
    ).astype(jnp.bfloat16)[:, :, :width]
    swap = [(i, (i + 1) % n_yh) for i in range(n_yh)]
    far_rows = lax.ppermute(outgoing, "yh", perm=swap)
    weight_far = lax.ppermute(weight_partner, "yh", perm=swap)

    hidden = saved_hidden.reshape(exp_devices, most, hidden_units)
    plane = lambda x, p: lax.dynamic_slice_in_dim(x, p * n_z, n_z, axis=0)
    near_hidden = plane(hidden, yh).reshape(n_z * most, hidden_units)
    far_hidden = plane(hidden, partner_yh).reshape(n_z * most, hidden_units)
    gathered_w = lax.all_gather(down_proj, "rep", axis=0, tiled=True).reshape(
        hidden_units, width
    )

    def expert_side(rows, row_weight, hid):
        rows = rows.reshape(n_z * most, width)
        scale = row_weight.reshape(n_z * most, 1)
        projected = jnp.einsum(
            "rd,hd->rh", rows, gathered_w, preferred_element_type=jnp.float32
        )
        hidden_grad = (scale * projected).astype(jnp.bfloat16)
        combine = ROUTE_SCALE * jnp.sum(hid.astype(jnp.float32) * projected, axis=-1)
        scaled = (scale * rows.astype(jnp.float32)).astype(jnp.bfloat16)
        term = jnp.einsum("rh,rd->hd", hid, scaled, preferred_element_type=jnp.float32)
        return hidden_grad, combine, term

    near_grad, near_combine, near_term = expert_side(near_rows, weight_mine, near_hidden)
    far_grad, far_combine, far_term = expert_side(far_rows, weight_far, far_hidden)
    grad_term = near_term + far_term
    down_grad = lax.psum_scatter(
        grad_term.astype(jnp.bfloat16), "rep", scatter_dimension=0, tiled=True
    ).astype(jnp.float32)

    first = yh == 0
    hidden_grad = jnp.where(
        first,
        jnp.concatenate([near_grad, far_grad], axis=0),
        jnp.concatenate([far_grad, near_grad], axis=0),
    )
    combine_grad = jnp.where(
        first,
        jnp.concatenate([near_combine, far_combine], axis=0),
        jnp.concatenate([far_combine, near_combine], axis=0),
    ).reshape(exp_devices, most)
    returned = lax.all_to_all(
        combine_grad, ("yh", "z"), split_axis=0, concat_axis=0, tiled=True
    )
    expert_ids = jnp.arange(expert_count, dtype=jnp.int32)
    slot_ids = jnp.arange(most, dtype=jnp.float32)
    by_expert = jnp.sum(
        jnp.where((routes[:, :, None] == expert_ids)[:, :, :, None], returned[None, None], 0.0),
        axis=2,
    )
    route_grad = jnp.sum(
        jnp.where(slots[:, :, None] == slot_ids, by_expert, 0.0), axis=2
    )
    affinity_grad = (route_grad - jnp.sum(route_grad * shares, axis=-1, keepdims=True)) / totals
    return (
        affinity_grad,
        hidden_grad.reshape(saved_hidden.shape),
        down_grad.reshape(down_proj.shape),
    )


def solution(mesh):
    n_exp = mesh.shape["exp"]
    n_yh = 2
    split = Mesh(
        mesh.devices.reshape(mesh.shape["rep"], n_yh, n_exp // n_yh),
        ("rep", "yh", "z"),
    )
    return jax.shard_map(
        on_device,
        mesh=split,
        in_specs=(
            P(TOKENS_SPEC, None),
            P(TOKENS_SPEC, None),
            P(TOKENS_SPEC, None),
            P("rep", ("yh", "z"), None, None, None),
            P("rep", ("yh", "z"), None),
        ),
        out_specs=(
            P(TOKENS_SPEC, None),
            P("rep", ("yh", "z"), None, None, None),
            P("rep", ("yh", "z"), None),
        ),
        check_vma=False,
    )
```

```python
import jax
import jax.numpy as jnp
from jax import lax
from jax.experimental import pallas as pl
from jax.experimental.pallas import tpu as pltpu
from jax.sharding import Mesh
from jax.sharding import PartitionSpec as P

ROUTE_SCALE = 2.5
TOKENS_SPEC = ("rep", "yh", "z")
META = 128
MESH_ID = pl.DeviceIdType.MESH


def gather_weight_kernel(n, w_ref, out_ref, send_sem, recv_sem, local_sem):
    me = lax.axis_index("rep")
    yh = lax.axis_index("yh")
    z = lax.axis_index("z")
    barrier = pltpu.get_barrier_semaphore()
    for off in range(1, n):
        peer = lax.rem(me + off, n)
        pl.semaphore_signal(barrier, inc=1, device_id=(peer, yh, z), device_id_type=MESH_ID)
    pl.semaphore_wait(barrier, n - 1)
    local = pltpu.make_async_copy(w_ref, out_ref.at[me], local_sem)
    local.start()
    sends = []
    for off in range(1, n):
        peer = lax.rem(me + off, n)
        copy = pltpu.make_async_remote_copy(
            src_ref=w_ref,
            dst_ref=out_ref.at[me],
            send_sem=send_sem.at[off],
            recv_sem=recv_sem.at[off],
            device_id=(peer, yh, z),
            device_id_type=MESH_ID,
        )
        copy.start()
        sends.append(copy)
    for copy in sends:
        copy.wait_send()
    for off in range(1, n):
        source = lax.rem(me - off + n, n)
        incoming = pltpu.make_async_remote_copy(
            src_ref=w_ref,
            dst_ref=out_ref.at[source],
            send_sem=send_sem.at[off],
            recv_sem=recv_sem.at[off],
            device_id=(source, yh, z),
            device_id_type=MESH_ID,
        )
        incoming.wait_recv()
    local.wait()


def gather_weight(w):
    n = lax.axis_size("rep")
    rows, width = w.shape
    return pl.pallas_call(
        lambda *refs: gather_weight_kernel(n, *refs),
        out_shape=jax.ShapeDtypeStruct((n, rows, width), w.dtype),
        in_specs=[pl.BlockSpec(memory_space=pl.ANY)],
        out_specs=pl.BlockSpec(memory_space=pl.ANY),
        scratch_shapes=[
            pltpu.SemaphoreType.DMA((n,)),
            pltpu.SemaphoreType.DMA((n,)),
            pltpu.SemaphoreType.DMA(()),
        ],
        compiler_params=pltpu.CompilerParams(collective_id=0, has_side_effects=True),
        cost_estimate=pl.CostEstimate(
            flops=0, transcendentals=0, bytes_accessed=2 * n * rows * width * w.dtype.itemsize
        ),
    )(w)


def local_slots(routes, expert_count):
    tok = routes.shape[0]
    expert_ids = jnp.arange(expert_count, dtype=jnp.int32)
    hits = routes[:, :, None] == expert_ids
    naming = jnp.sum(hits.astype(jnp.float32), axis=1)
    earlier = (
        jnp.arange(tok, dtype=jnp.int32)[None, :] < jnp.arange(tok, dtype=jnp.int32)[:, None]
    ).astype(jnp.bfloat16)
    before = jnp.dot(earlier, naming.astype(jnp.bfloat16), preferred_element_type=jnp.float32)
    return jnp.sum(jnp.where(hits, before[:, None, :], 0.0), axis=2)


def selection(route_f, slot_f, weight_f, expert, most):
    names = route_f == expert.astype(jnp.float32)
    position = jnp.sum(jnp.where(names, slot_f + 1.0, 0.0), axis=2) - 1.0
    weight = jnp.sum(jnp.where(names, weight_f, 0.0), axis=2)
    picks = position[:, None, :] == jnp.arange(most, dtype=jnp.float32)[None, :, None]
    packed_weight = jnp.sum(jnp.where(picks, weight[:, None, :], 0.0), axis=2)
    return picks.astype(jnp.bfloat16), packed_weight


def on_device(grad_out, routes, affinity, saved_hidden, down_proj):
    n_yh = lax.axis_size("yh")
    n_z = lax.axis_size("z")
    exp_devices = n_yh * n_z
    local_experts = down_proj.shape[1]
    expert_count = exp_devices * local_experts
    most = saved_hidden.shape[3]
    width = grad_out.shape[1]
    hidden_units = saved_hidden.shape[4]
    topk = routes.shape[1]
    yh = lax.axis_index("yh")
    z = lax.axis_index("z")
    partner_yh = (yh + 1) % n_yh
    mine = yh * n_z + z
    partner = partner_yh * n_z + z

    totals = jnp.sum(affinity, axis=-1, keepdims=True)
    shares = affinity / totals
    route_weight = (ROUTE_SCALE * shares).astype(jnp.bfloat16)
    slots = local_slots(routes, expert_count)
    meta = jnp.concatenate(
        [
            routes.astype(jnp.bfloat16),
            slots.astype(jnp.bfloat16),
            route_weight,
            jnp.zeros((routes.shape[0], META - 3 * topk), jnp.bfloat16),
        ],
        axis=1,
    )
    carried = jnp.concatenate([grad_out, meta], axis=1)
    gathered = lax.all_gather(carried, "z", axis=0, tiled=False)
    gathered_w = gather_weight(down_proj.reshape(-1, width)).reshape(hidden_units, width)
    gathered, gathered_w = lax.optimization_barrier((gathered, gathered_w))
    meta_all = gathered[:, :, width : width + 3 * topk].astype(jnp.float32)
    route_f = meta_all[:, :, 0:topk]
    slot_f = meta_all[:, :, topk : 2 * topk]
    weight_f = meta_all[:, :, 2 * topk : 3 * topk]

    pick_mine, weight_mine = selection(route_f, slot_f, weight_f, mine, most)
    pick_partner, weight_partner = selection(route_f, slot_f, weight_f, partner, most)
    near_rows = jnp.einsum(
        "sjt,std->sjd", pick_mine, gathered, preferred_element_type=jnp.float32
    ).astype(jnp.bfloat16)[:, :, :width]
    outgoing = jnp.einsum(
        "sjt,std->sjd", pick_partner, gathered, preferred_element_type=jnp.float32
    ).astype(jnp.bfloat16)[:, :, :width]
    swap = [(i, (i + 1) % n_yh) for i in range(n_yh)]
    far_rows = lax.ppermute(outgoing, "yh", perm=swap)
    weight_far = lax.ppermute(weight_partner, "yh", perm=swap)

    hidden = saved_hidden.reshape(exp_devices, most, hidden_units)
    plane = lambda x, p: lax.dynamic_slice_in_dim(x, p * n_z, n_z, axis=0)
    near_hidden = plane(hidden, yh).reshape(n_z * most, hidden_units)
    far_hidden = plane(hidden, partner_yh).reshape(n_z * most, hidden_units)

    def expert_side(rows, row_weight, hid):
        rows = rows.reshape(n_z * most, width)
        scale = row_weight.reshape(n_z * most, 1)
        projected = jnp.einsum(
            "rd,hd->rh", rows, gathered_w, preferred_element_type=jnp.float32
        )
        hidden_grad = (scale * projected).astype(jnp.bfloat16)
        combine = ROUTE_SCALE * jnp.sum(hid.astype(jnp.float32) * projected, axis=-1)
        scaled = (scale * rows.astype(jnp.float32)).astype(jnp.bfloat16)
        term = jnp.einsum("rh,rd->hd", hid, scaled, preferred_element_type=jnp.float32)
        return hidden_grad, combine, term

    near_grad, near_combine, near_term = expert_side(near_rows, weight_mine, near_hidden)
    far_grad, far_combine, far_term = expert_side(far_rows, weight_far, far_hidden)
    grad_term = near_term + far_term
    down_grad = lax.psum_scatter(
        grad_term.astype(jnp.bfloat16), "rep", scatter_dimension=0, tiled=True
    ).astype(jnp.float32)

    first = yh == 0
    hidden_grad = jnp.where(
        first,
        jnp.concatenate([near_grad, far_grad], axis=0),
        jnp.concatenate([far_grad, near_grad], axis=0),
    )
    combine_grad = jnp.where(
        first,
        jnp.concatenate([near_combine, far_combine], axis=0),
        jnp.concatenate([far_combine, near_combine], axis=0),
    ).reshape(exp_devices, most)
    returned = lax.all_to_all(
        combine_grad, ("yh", "z"), split_axis=0, concat_axis=0, tiled=True
    )
    expert_ids = jnp.arange(expert_count, dtype=jnp.int32)
    slot_ids = jnp.arange(most, dtype=jnp.float32)
    by_expert = jnp.sum(
        jnp.where((routes[:, :, None] == expert_ids)[:, :, :, None], returned[None, None], 0.0),
        axis=2,
    )
    route_grad = jnp.sum(
        jnp.where(slots[:, :, None] == slot_ids, by_expert, 0.0), axis=2
    )
    affinity_grad = (route_grad - jnp.sum(route_grad * shares, axis=-1, keepdims=True)) / totals
    return (
        affinity_grad,
        hidden_grad.reshape(saved_hidden.shape),
        down_grad.reshape(down_proj.shape),
    )


def solution(mesh):
    n_exp = mesh.shape["exp"]
    n_yh = 2
    split = Mesh(
        mesh.devices.reshape(mesh.shape["rep"], n_yh, n_exp // n_yh),
        ("rep", "yh", "z"),
    )
    return jax.shard_map(
        on_device,
        mesh=split,
        in_specs=(
            P(TOKENS_SPEC, None),
            P(TOKENS_SPEC, None),
            P(TOKENS_SPEC, None),
            P("rep", ("yh", "z"), None, None, None),
            P("rep", ("yh", "z"), None),
        ),
        out_specs=(
            P(TOKENS_SPEC, None),
            P("rep", ("yh", "z"), None, None, None),
            P("rep", ("yh", "z"), None),
        ),
        check_vma=False,
    )
```

```python
import jax
import jax.numpy as jnp
from jax import lax
from jax.experimental import pallas as pl
from jax.experimental.pallas import tpu as pltpu
from jax.sharding import Mesh
from jax.sharding import PartitionSpec as P

ROUTE_SCALE = 2.5
TOKENS_SPEC = ("rep", "yh", "z")
META = 128
MESH_ID = pl.DeviceIdType.MESH


def gather_weight_kernel(n, w_ref, out_ref, send_sem, recv_sem, fwd_send, fwd_recv, own_sem, local_sem):
    me = lax.axis_index("rep")
    yh = lax.axis_index("yh")
    z = lax.axis_index("z")
    chips = n // 2
    chip = me // 2
    core = me % 2
    partner = chip * 2 + (1 - core)
    barrier = pltpu.get_barrier_semaphore()
    for off in range(1, chips):
        peer = lax.rem(chip + off, chips) * 2 + core
        pl.semaphore_signal(barrier, inc=1, device_id=(peer, yh, z), device_id_type=MESH_ID)
    pl.semaphore_signal(barrier, inc=1, device_id=(partner, yh, z), device_id_type=MESH_ID)
    pl.semaphore_wait(barrier, chips)
    local = pltpu.make_async_copy(w_ref, out_ref.at[me], local_sem)
    local.start()
    own = pltpu.make_async_remote_copy(
        src_ref=w_ref,
        dst_ref=out_ref.at[me],
        send_sem=own_sem.at[0],
        recv_sem=own_sem.at[1],
        device_id=(partner, yh, z),
        device_id_type=MESH_ID,
    )
    own.start()
    sends = []
    for off in range(1, chips):
        peer = lax.rem(chip + off, chips) * 2 + core
        copy = pltpu.make_async_remote_copy(
            src_ref=w_ref,
            dst_ref=out_ref.at[me],
            send_sem=send_sem.at[off],
            recv_sem=recv_sem.at[off],
            device_id=(peer, yh, z),
            device_id_type=MESH_ID,
        )
        copy.start()
        sends.append(copy)
    forwards = []
    for off in range(1, chips):
        source = lax.rem(chip - off + chips, chips) * 2 + core
        incoming = pltpu.make_async_remote_copy(
            src_ref=w_ref,
            dst_ref=out_ref.at[source],
            send_sem=send_sem.at[off],
            recv_sem=recv_sem.at[off],
            device_id=(source, yh, z),
            device_id_type=MESH_ID,
        )
        incoming.wait_recv()
        forward = pltpu.make_async_remote_copy(
            src_ref=out_ref.at[source],
            dst_ref=out_ref.at[source],
            send_sem=fwd_send.at[off],
            recv_sem=fwd_recv.at[off],
            device_id=(partner, yh, z),
            device_id_type=MESH_ID,
        )
        forward.start()
        forwards.append(forward)
    for copy in sends:
        copy.wait_send()
    own.wait_send()
    for forward in forwards:
        forward.wait_send()
    partner_own = pltpu.make_async_remote_copy(
        src_ref=w_ref,
        dst_ref=out_ref.at[partner],
        send_sem=own_sem.at[0],
        recv_sem=own_sem.at[1],
        device_id=(partner, yh, z),
        device_id_type=MESH_ID,
    )
    partner_own.wait_recv()
    for off in range(1, chips):
        source = lax.rem(chip - off + chips, chips) * 2 + (1 - core)
        relayed = pltpu.make_async_remote_copy(
            src_ref=out_ref.at[source],
            dst_ref=out_ref.at[source],
            send_sem=fwd_send.at[off],
            recv_sem=fwd_recv.at[off],
            device_id=(partner, yh, z),
            device_id_type=MESH_ID,
        )
        relayed.wait_recv()
    local.wait()


def gather_weight(w):
    n = lax.axis_size("rep")
    rows, width = w.shape
    return pl.pallas_call(
        lambda *refs: gather_weight_kernel(n, *refs),
        out_shape=jax.ShapeDtypeStruct((n, rows, width), w.dtype),
        in_specs=[pl.BlockSpec(memory_space=pl.ANY)],
        out_specs=pl.BlockSpec(memory_space=pl.ANY),
        scratch_shapes=[
            pltpu.SemaphoreType.DMA((n // 2,)),
            pltpu.SemaphoreType.DMA((n // 2,)),
            pltpu.SemaphoreType.DMA((n // 2,)),
            pltpu.SemaphoreType.DMA((n // 2,)),
            pltpu.SemaphoreType.DMA((2,)),
            pltpu.SemaphoreType.DMA(()),
        ],
        compiler_params=pltpu.CompilerParams(collective_id=0, has_side_effects=True),
        cost_estimate=pl.CostEstimate(
            flops=0, transcendentals=0, bytes_accessed=2 * n * rows * width * w.dtype.itemsize
        ),
    )(w)


def local_slots(routes, expert_count):
    tok = routes.shape[0]
    expert_ids = jnp.arange(expert_count, dtype=jnp.int32)
    hits = routes[:, :, None] == expert_ids
    naming = jnp.sum(hits.astype(jnp.float32), axis=1)
    earlier = (
        jnp.arange(tok, dtype=jnp.int32)[None, :] < jnp.arange(tok, dtype=jnp.int32)[:, None]
    ).astype(jnp.bfloat16)
    before = jnp.dot(earlier, naming.astype(jnp.bfloat16), preferred_element_type=jnp.float32)
    return jnp.sum(jnp.where(hits, before[:, None, :], 0.0), axis=2)


def selection(route_f, slot_f, weight_f, expert, most):
    names = route_f == expert.astype(jnp.float32)
    position = jnp.sum(jnp.where(names, slot_f + 1.0, 0.0), axis=2) - 1.0
    weight = jnp.sum(jnp.where(names, weight_f, 0.0), axis=2)
    picks = position[:, None, :] == jnp.arange(most, dtype=jnp.float32)[None, :, None]
    packed_weight = jnp.sum(jnp.where(picks, weight[:, None, :], 0.0), axis=2)
    return picks.astype(jnp.bfloat16), packed_weight


def on_device(grad_out, routes, affinity, saved_hidden, down_proj):
    n_yh = lax.axis_size("yh")
    n_z = lax.axis_size("z")
    exp_devices = n_yh * n_z
    local_experts = down_proj.shape[1]
    expert_count = exp_devices * local_experts
    most = saved_hidden.shape[3]
    width = grad_out.shape[1]
    hidden_units = saved_hidden.shape[4]
    topk = routes.shape[1]
    yh = lax.axis_index("yh")
    z = lax.axis_index("z")
    partner_yh = (yh + 1) % n_yh
    mine = yh * n_z + z
    partner = partner_yh * n_z + z

    totals = jnp.sum(affinity, axis=-1, keepdims=True)
    shares = affinity / totals
    route_weight = (ROUTE_SCALE * shares).astype(jnp.bfloat16)
    slots = local_slots(routes, expert_count)
    meta = jnp.concatenate(
        [
            routes.astype(jnp.bfloat16),
            slots.astype(jnp.bfloat16),
            route_weight,
            jnp.zeros((routes.shape[0], META - 3 * topk), jnp.bfloat16),
        ],
        axis=1,
    )
    carried = jnp.concatenate([grad_out, meta], axis=1)
    gathered = lax.all_gather(carried, "z", axis=0, tiled=False)
    gathered_w = gather_weight(down_proj.reshape(-1, width)).reshape(hidden_units, width)
    gathered, gathered_w = lax.optimization_barrier((gathered, gathered_w))
    meta_all = gathered[:, :, width : width + 3 * topk].astype(jnp.float32)
    route_f = meta_all[:, :, 0:topk]
    slot_f = meta_all[:, :, topk : 2 * topk]
    weight_f = meta_all[:, :, 2 * topk : 3 * topk]

    pick_mine, weight_mine = selection(route_f, slot_f, weight_f, mine, most)
    pick_partner, weight_partner = selection(route_f, slot_f, weight_f, partner, most)
    near_rows = jnp.einsum(
        "sjt,std->sjd", pick_mine, gathered, preferred_element_type=jnp.float32
    ).astype(jnp.bfloat16)[:, :, :width]
    outgoing = jnp.einsum(
        "sjt,std->sjd", pick_partner, gathered, preferred_element_type=jnp.float32
    ).astype(jnp.bfloat16)[:, :, :width]
    swap = [(i, (i + 1) % n_yh) for i in range(n_yh)]
    far_rows = lax.ppermute(outgoing, "yh", perm=swap)
    weight_far = lax.ppermute(weight_partner, "yh", perm=swap)

    hidden = saved_hidden.reshape(exp_devices, most, hidden_units)
    plane = lambda x, p: lax.dynamic_slice_in_dim(x, p * n_z, n_z, axis=0)
    near_hidden = plane(hidden, yh).reshape(n_z * most, hidden_units)
    far_hidden = plane(hidden, partner_yh).reshape(n_z * most, hidden_units)

    def expert_side(rows, row_weight, hid):
        rows = rows.reshape(n_z * most, width)
        scale = row_weight.reshape(n_z * most, 1)
        projected = jnp.einsum(
            "rd,hd->rh", rows, gathered_w, preferred_element_type=jnp.float32
        )
        hidden_grad = (scale * projected).astype(jnp.bfloat16)
        combine = ROUTE_SCALE * jnp.sum(hid.astype(jnp.float32) * projected, axis=-1)
        scaled = (scale * rows.astype(jnp.float32)).astype(jnp.bfloat16)
        term = jnp.einsum("rh,rd->hd", hid, scaled, preferred_element_type=jnp.float32)
        return hidden_grad, combine, term

    near_grad, near_combine, near_term = expert_side(near_rows, weight_mine, near_hidden)
    far_grad, far_combine, far_term = expert_side(far_rows, weight_far, far_hidden)
    grad_term = near_term + far_term
    down_grad = lax.psum_scatter(
        grad_term.astype(jnp.bfloat16), "rep", scatter_dimension=0, tiled=True
    ).astype(jnp.float32)

    first = yh == 0
    hidden_grad = jnp.where(
        first,
        jnp.concatenate([near_grad, far_grad], axis=0),
        jnp.concatenate([far_grad, near_grad], axis=0),
    )
    combine_grad = jnp.where(
        first,
        jnp.concatenate([near_combine, far_combine], axis=0),
        jnp.concatenate([far_combine, near_combine], axis=0),
    ).reshape(exp_devices, most)
    returned = lax.all_to_all(
        combine_grad, ("yh", "z"), split_axis=0, concat_axis=0, tiled=True
    )
    expert_ids = jnp.arange(expert_count, dtype=jnp.int32)
    slot_ids = jnp.arange(most, dtype=jnp.float32)
    by_expert = jnp.sum(
        jnp.where((routes[:, :, None] == expert_ids)[:, :, :, None], returned[None, None], 0.0),
        axis=2,
    )
    route_grad = jnp.sum(
        jnp.where(slots[:, :, None] == slot_ids, by_expert, 0.0), axis=2
    )
    affinity_grad = (route_grad - jnp.sum(route_grad * shares, axis=-1, keepdims=True)) / totals
    return (
        affinity_grad,
        hidden_grad.reshape(saved_hidden.shape),
        down_grad.reshape(down_proj.shape),
    )


def solution(mesh):
    n_exp = mesh.shape["exp"]
    n_yh = 2
    split = Mesh(
        mesh.devices.reshape(mesh.shape["rep"], n_yh, n_exp // n_yh),
        ("rep", "yh", "z"),
    )
    return jax.shard_map(
        on_device,
        mesh=split,
        in_specs=(
            P(TOKENS_SPEC, None),
            P(TOKENS_SPEC, None),
            P(TOKENS_SPEC, None),
            P("rep", ("yh", "z"), None, None, None),
            P("rep", ("yh", "z"), None),
        ),
        out_specs=(
            P(TOKENS_SPEC, None),
            P("rep", ("yh", "z"), None, None, None),
            P("rep", ("yh", "z"), None),
        ),
        check_vma=False,
    )
```

```python
import jax
import jax.numpy as jnp
from jax import lax
from jax.experimental import pallas as pl
from jax.experimental.pallas import tpu as pltpu
from jax.sharding import Mesh
from jax.sharding import PartitionSpec as P

ROUTE_SCALE = 2.5
TOKENS_SPEC = ("rep", "yh", "z")
META = 128
MESH_ID = pl.DeviceIdType.MESH


def gather_weight_kernel(n, w_ref, out_ref, send_sem, recv_sem, fwd_send, fwd_recv, own_sem, local_sem):
    me = lax.axis_index("rep")
    yh = lax.axis_index("yh")
    z = lax.axis_index("z")
    chips = n // 2
    chip = me // 2
    core = me % 2
    partner = chip * 2 + (1 - core)
    barrier = pltpu.get_barrier_semaphore()
    for off in range(1, chips):
        peer = lax.rem(chip + off, chips) * 2 + core
        pl.semaphore_signal(barrier, inc=1, device_id=(peer, yh, z), device_id_type=MESH_ID)
    pl.semaphore_signal(barrier, inc=1, device_id=(partner, yh, z), device_id_type=MESH_ID)
    pl.semaphore_wait(barrier, chips)
    local = pltpu.make_async_copy(w_ref, out_ref.at[me], local_sem)
    local.start()
    own = pltpu.make_async_remote_copy(
        src_ref=w_ref,
        dst_ref=out_ref.at[me],
        send_sem=own_sem.at[0],
        recv_sem=own_sem.at[1],
        device_id=(partner, yh, z),
        device_id_type=MESH_ID,
    )
    own.start()
    sends = []
    for off in range(1, chips):
        peer = lax.rem(chip + off, chips) * 2 + core
        copy = pltpu.make_async_remote_copy(
            src_ref=w_ref,
            dst_ref=out_ref.at[me],
            send_sem=send_sem.at[off],
            recv_sem=recv_sem.at[off],
            device_id=(peer, yh, z),
            device_id_type=MESH_ID,
        )
        copy.start()
        sends.append(copy)
    forwards = []
    for off in range(1, chips):
        source = lax.rem(chip - off + chips, chips) * 2 + core
        incoming = pltpu.make_async_remote_copy(
            src_ref=w_ref,
            dst_ref=out_ref.at[source],
            send_sem=send_sem.at[off],
            recv_sem=recv_sem.at[off],
            device_id=(source, yh, z),
            device_id_type=MESH_ID,
        )
        incoming.wait_recv()
        forward = pltpu.make_async_remote_copy(
            src_ref=out_ref.at[source],
            dst_ref=out_ref.at[source],
            send_sem=fwd_send.at[off],
            recv_sem=fwd_recv.at[off],
            device_id=(partner, yh, z),
            device_id_type=MESH_ID,
        )
        forward.start()
        forwards.append(forward)
    for copy in sends:
        copy.wait_send()
    own.wait_send()
    for forward in forwards:
        forward.wait_send()
    partner_own = pltpu.make_async_remote_copy(
        src_ref=w_ref,
        dst_ref=out_ref.at[partner],
        send_sem=own_sem.at[0],
        recv_sem=own_sem.at[1],
        device_id=(partner, yh, z),
        device_id_type=MESH_ID,
    )
    partner_own.wait_recv()
    for off in range(1, chips):
        source = lax.rem(chip - off + chips, chips) * 2 + (1 - core)
        relayed = pltpu.make_async_remote_copy(
            src_ref=out_ref.at[source],
            dst_ref=out_ref.at[source],
            send_sem=fwd_send.at[off],
            recv_sem=fwd_recv.at[off],
            device_id=(partner, yh, z),
            device_id_type=MESH_ID,
        )
        relayed.wait_recv()
    local.wait()


def gather_weight(w, cid):
    n = lax.axis_size("rep")
    rows, width = w.shape
    return pl.pallas_call(
        lambda *refs: gather_weight_kernel(n, *refs),
        out_shape=jax.ShapeDtypeStruct((n, rows, width), w.dtype),
        in_specs=[pl.BlockSpec(memory_space=pl.ANY)],
        out_specs=pl.BlockSpec(memory_space=pl.ANY),
        scratch_shapes=[
            pltpu.SemaphoreType.DMA((n // 2,)),
            pltpu.SemaphoreType.DMA((n // 2,)),
            pltpu.SemaphoreType.DMA((n // 2,)),
            pltpu.SemaphoreType.DMA((n // 2,)),
            pltpu.SemaphoreType.DMA((2,)),
            pltpu.SemaphoreType.DMA(()),
        ],
        compiler_params=pltpu.CompilerParams(collective_id=cid, has_side_effects=True),
        cost_estimate=pl.CostEstimate(
            flops=0, transcendentals=0, bytes_accessed=2 * n * rows * width * w.dtype.itemsize
        ),
    )(w)


def local_slots(routes, expert_count):
    tok = routes.shape[0]
    expert_ids = jnp.arange(expert_count, dtype=jnp.int32)
    hits = routes[:, :, None] == expert_ids
    naming = jnp.sum(hits.astype(jnp.float32), axis=1)
    earlier = (
        jnp.arange(tok, dtype=jnp.int32)[None, :] < jnp.arange(tok, dtype=jnp.int32)[:, None]
    ).astype(jnp.bfloat16)
    before = jnp.dot(earlier, naming.astype(jnp.bfloat16), preferred_element_type=jnp.float32)
    return jnp.sum(jnp.where(hits, before[:, None, :], 0.0), axis=2)


def selection(route_f, slot_f, weight_f, expert, most):
    names = route_f == expert.astype(jnp.float32)
    position = jnp.sum(jnp.where(names, slot_f + 1.0, 0.0), axis=2) - 1.0
    weight = jnp.sum(jnp.where(names, weight_f, 0.0), axis=2)
    picks = position[:, None, :] == jnp.arange(most, dtype=jnp.float32)[None, :, None]
    packed_weight = jnp.sum(jnp.where(picks, weight[:, None, :], 0.0), axis=2)
    return picks.astype(jnp.bfloat16), packed_weight


def block_picks(picks):
    sources, most, tok = picks.shape
    eye = jnp.eye(sources, dtype=picks.dtype)
    return (picks[:, :, None, :] * eye[:, None, :, None]).reshape(sources * most, sources * tok)


def on_device(grad_out, routes, affinity, saved_hidden, down_proj):
    n_yh = lax.axis_size("yh")
    n_z = lax.axis_size("z")
    exp_devices = n_yh * n_z
    local_experts = down_proj.shape[1]
    expert_count = exp_devices * local_experts
    most = saved_hidden.shape[3]
    width = grad_out.shape[1]
    hidden_units = saved_hidden.shape[4]
    topk = routes.shape[1]
    tok = routes.shape[0]
    yh = lax.axis_index("yh")
    z = lax.axis_index("z")
    partner_yh = (yh + 1) % n_yh
    mine = yh * n_z + z
    partner = partner_yh * n_z + z
    half = width // 2
    swap = [(i, (i + 1) % n_yh) for i in range(n_yh)]

    totals = jnp.sum(affinity, axis=-1, keepdims=True)
    shares = affinity / totals
    route_weight = (ROUTE_SCALE * shares).astype(jnp.bfloat16)
    slots = local_slots(routes, expert_count)
    meta = jnp.concatenate(
        [
            routes.astype(jnp.bfloat16),
            slots.astype(jnp.bfloat16),
            route_weight,
            jnp.zeros((tok, META - 3 * topk), jnp.bfloat16),
        ],
        axis=1,
    )
    first_part = jnp.concatenate([grad_out[:, :half], meta], axis=1)
    gathered_a = lax.all_gather(first_part, "z", axis=0, tiled=True)
    weight_rows = down_proj.reshape(-1, width)
    w_a = gather_weight(weight_rows[:, :half], 0).reshape(hidden_units, half)
    gathered_a, w_a = lax.optimization_barrier((gathered_a, w_a))
    meta_all = gathered_a[:, half : half + 3 * topk].astype(jnp.float32).reshape(n_z, tok, 3 * topk)
    route_f = meta_all[:, :, 0:topk]
    slot_f = meta_all[:, :, topk : 2 * topk]
    weight_f = meta_all[:, :, 2 * topk : 3 * topk]
    pick_mine, weight_mine = selection(route_f, slot_f, weight_f, mine, most)
    pick_partner, weight_partner = selection(route_f, slot_f, weight_f, partner, most)
    pick_mine = block_picks(pick_mine)
    pick_partner = block_picks(pick_partner)
    weight_far = lax.ppermute(weight_partner, "yh", perm=swap)

    def pack(gathered):
        near = jnp.dot(pick_mine, gathered, preferred_element_type=jnp.float32)
        out = jnp.dot(pick_partner, gathered, preferred_element_type=jnp.float32)
        far = lax.ppermute(out.astype(jnp.bfloat16), "yh", perm=swap)
        return near.astype(jnp.bfloat16), far

    near_a, far_a = pack(gathered_a)
    second_part, _ = lax.optimization_barrier((grad_out[:, half:], gathered_a))
    gathered_b = lax.all_gather(second_part, "z", axis=0, tiled=True)
    w_b = gather_weight(weight_rows[:, half:], 1).reshape(hidden_units, width - half)
    far_a, w_b = lax.optimization_barrier((far_a, w_b))
    near_b, far_b = pack(gathered_b)

    hidden = saved_hidden.reshape(exp_devices, most, hidden_units)
    plane = lambda x, p: lax.dynamic_slice_in_dim(x, p * n_z, n_z, axis=0)
    near_hidden = plane(hidden, yh).reshape(n_z * most, hidden_units)
    far_hidden = plane(hidden, partner_yh).reshape(n_z * most, hidden_units)
    near_scale = weight_mine.reshape(n_z * most, 1)
    far_scale = weight_far.reshape(n_z * most, 1)

    def columns(rows, scale, hid, w_cols):
        projected = jnp.einsum(
            "rd,hd->rh", rows[:, :half], w_cols, preferred_element_type=jnp.float32
        )
        scaled = (scale * rows[:, :half].astype(jnp.float32)).astype(jnp.bfloat16)
        term = jnp.einsum("rh,rd->hd", hid, scaled, preferred_element_type=jnp.float32)
        return projected, term

    proj_na, term_na = columns(near_a, near_scale, near_hidden, w_a)
    proj_fa, term_fa = columns(far_a, far_scale, far_hidden, w_a)
    grad_a = lax.psum_scatter(
        (term_na + term_fa).astype(jnp.bfloat16), "rep", scatter_dimension=0, tiled=True
    )
    proj_nb, term_nb = columns(near_b, near_scale, near_hidden, w_b)
    proj_fb, term_fb = columns(far_b, far_scale, far_hidden, w_b)
    grad_b = lax.psum_scatter(
        (term_nb + term_fb).astype(jnp.bfloat16), "rep", scatter_dimension=0, tiled=True
    )
    down_grad = jnp.concatenate([grad_a, grad_b], axis=1).astype(jnp.float32)

    near_proj = proj_na + proj_nb
    far_proj = proj_fa + proj_fb
    near_grad = (near_scale * near_proj).astype(jnp.bfloat16)
    far_grad = (far_scale * far_proj).astype(jnp.bfloat16)
    near_combine = ROUTE_SCALE * jnp.sum(near_hidden.astype(jnp.float32) * near_proj, axis=-1)
    far_combine = ROUTE_SCALE * jnp.sum(far_hidden.astype(jnp.float32) * far_proj, axis=-1)

    first = yh == 0
    hidden_grad = jnp.where(
        first,
        jnp.concatenate([near_grad, far_grad], axis=0),
        jnp.concatenate([far_grad, near_grad], axis=0),
    )
    combine_grad = jnp.where(
        first,
        jnp.concatenate([near_combine, far_combine], axis=0),
        jnp.concatenate([far_combine, near_combine], axis=0),
    ).reshape(exp_devices, most)
    returned = lax.all_to_all(
        combine_grad, ("yh", "z"), split_axis=0, concat_axis=0, tiled=True
    )
    expert_ids = jnp.arange(expert_count, dtype=jnp.int32)
    slot_ids = jnp.arange(most, dtype=jnp.float32)
    by_expert = jnp.sum(
        jnp.where((routes[:, :, None] == expert_ids)[:, :, :, None], returned[None, None], 0.0),
        axis=2,
    )
    route_grad = jnp.sum(
        jnp.where(slots[:, :, None] == slot_ids, by_expert, 0.0), axis=2
    )
    affinity_grad = (route_grad - jnp.sum(route_grad * shares, axis=-1, keepdims=True)) / totals
    return (
        affinity_grad,
        hidden_grad.reshape(saved_hidden.shape),
        down_grad.reshape(down_proj.shape),
    )


def solution(mesh):
    n_exp = mesh.shape["exp"]
    n_yh = 2
    split = Mesh(
        mesh.devices.reshape(mesh.shape["rep"], n_yh, n_exp // n_yh),
        ("rep", "yh", "z"),
    )
    return jax.shard_map(
        on_device,
        mesh=split,
        in_specs=(
            P(TOKENS_SPEC, None),
            P(TOKENS_SPEC, None),
            P(TOKENS_SPEC, None),
            P("rep", ("yh", "z"), None, None, None),
            P("rep", ("yh", "z"), None),
        ),
        out_specs=(
            P(TOKENS_SPEC, None),
            P("rep", ("yh", "z"), None, None, None),
            P("rep", ("yh", "z"), None),
        ),
        check_vma=False,
    )
```

```python
import jax
import jax.numpy as jnp
from jax import lax
from jax.experimental import pallas as pl
from jax.experimental.pallas import tpu as pltpu
from jax.sharding import Mesh
from jax.sharding import PartitionSpec as P

ROUTE_SCALE = 2.5
TOKENS_SPEC = ("rep", "yh", "z")
META = 128
MESH_ID = pl.DeviceIdType.MESH


def gather_weight_kernel(n, w_ref, out_ref, send_sem, recv_sem, fwd_send, fwd_recv, own_sem, local_sem):
    me = lax.axis_index("rep")
    yh = lax.axis_index("yh")
    z = lax.axis_index("z")
    chips = n // 2
    chip = me // 2
    core = me % 2
    partner = chip * 2 + (1 - core)
    barrier = pltpu.get_barrier_semaphore()
    for off in range(1, chips):
        peer = lax.rem(chip + off, chips) * 2 + core
        pl.semaphore_signal(barrier, inc=1, device_id=(peer, yh, z), device_id_type=MESH_ID)
    pl.semaphore_signal(barrier, inc=1, device_id=(partner, yh, z), device_id_type=MESH_ID)
    pl.semaphore_wait(barrier, chips)
    local = pltpu.make_async_copy(w_ref, out_ref.at[me], local_sem)
    local.start()
    own = pltpu.make_async_remote_copy(
        src_ref=w_ref,
        dst_ref=out_ref.at[me],
        send_sem=own_sem.at[0],
        recv_sem=own_sem.at[1],
        device_id=(partner, yh, z),
        device_id_type=MESH_ID,
    )
    own.start()
    sends = []
    for off in range(1, chips):
        peer = lax.rem(chip + off, chips) * 2 + core
        copy = pltpu.make_async_remote_copy(
            src_ref=w_ref,
            dst_ref=out_ref.at[me],
            send_sem=send_sem.at[off],
            recv_sem=recv_sem.at[off],
            device_id=(peer, yh, z),
            device_id_type=MESH_ID,
        )
        copy.start()
        sends.append(copy)
    forwards = []
    for off in range(1, chips):
        source = lax.rem(chip - off + chips, chips) * 2 + core
        incoming = pltpu.make_async_remote_copy(
            src_ref=w_ref,
            dst_ref=out_ref.at[source],
            send_sem=send_sem.at[off],
            recv_sem=recv_sem.at[off],
            device_id=(source, yh, z),
            device_id_type=MESH_ID,
        )
        incoming.wait_recv()
        forward = pltpu.make_async_remote_copy(
            src_ref=out_ref.at[source],
            dst_ref=out_ref.at[source],
            send_sem=fwd_send.at[off],
            recv_sem=fwd_recv.at[off],
            device_id=(partner, yh, z),
            device_id_type=MESH_ID,
        )
        forward.start()
        forwards.append(forward)
    for copy in sends:
        copy.wait_send()
    own.wait_send()
    for forward in forwards:
        forward.wait_send()
    partner_own = pltpu.make_async_remote_copy(
        src_ref=w_ref,
        dst_ref=out_ref.at[partner],
        send_sem=own_sem.at[0],
        recv_sem=own_sem.at[1],
        device_id=(partner, yh, z),
        device_id_type=MESH_ID,
    )
    partner_own.wait_recv()
    for off in range(1, chips):
        source = lax.rem(chip - off + chips, chips) * 2 + (1 - core)
        relayed = pltpu.make_async_remote_copy(
            src_ref=out_ref.at[source],
            dst_ref=out_ref.at[source],
            send_sem=fwd_send.at[off],
            recv_sem=fwd_recv.at[off],
            device_id=(partner, yh, z),
            device_id_type=MESH_ID,
        )
        relayed.wait_recv()
    local.wait()


def gather_weight(w):
    n = lax.axis_size("rep")
    rows, width = w.shape
    return pl.pallas_call(
        lambda *refs: gather_weight_kernel(n, *refs),
        out_shape=jax.ShapeDtypeStruct((n, rows, width), w.dtype),
        in_specs=[pl.BlockSpec(memory_space=pl.ANY)],
        out_specs=pl.BlockSpec(memory_space=pl.ANY),
        scratch_shapes=[
            pltpu.SemaphoreType.DMA((n // 2,)),
            pltpu.SemaphoreType.DMA((n // 2,)),
            pltpu.SemaphoreType.DMA((n // 2,)),
            pltpu.SemaphoreType.DMA((n // 2,)),
            pltpu.SemaphoreType.DMA((2,)),
            pltpu.SemaphoreType.DMA(()),
        ],
        compiler_params=pltpu.CompilerParams(collective_id=0, has_side_effects=True),
        cost_estimate=pl.CostEstimate(
            flops=0, transcendentals=0, bytes_accessed=2 * n * rows * width * w.dtype.itemsize
        ),
    )(w)


def local_slots(routes, expert_count):
    tok = routes.shape[0]
    expert_ids = jnp.arange(expert_count, dtype=jnp.int32)
    hits = routes[:, :, None] == expert_ids
    naming = jnp.sum(hits.astype(jnp.float32), axis=1)
    earlier = (
        jnp.arange(tok, dtype=jnp.int32)[None, :] < jnp.arange(tok, dtype=jnp.int32)[:, None]
    ).astype(jnp.bfloat16)
    before = jnp.dot(earlier, naming.astype(jnp.bfloat16), preferred_element_type=jnp.float32)
    return jnp.sum(jnp.where(hits, before[:, None, :], 0.0), axis=2)


def selection(route_f, slot_f, weight_f, expert, most):
    names = route_f == expert.astype(jnp.float32)
    position = jnp.sum(jnp.where(names, slot_f + 1.0, 0.0), axis=2) - 1.0
    weight = jnp.sum(jnp.where(names, weight_f, 0.0), axis=2)
    picks = position[:, None, :] == jnp.arange(most, dtype=jnp.float32)[None, :, None]
    packed_weight = jnp.sum(jnp.where(picks, weight[:, None, :], 0.0), axis=2)
    return picks.astype(jnp.bfloat16), packed_weight


def block_picks(picks):
    sources, most, tok = picks.shape
    eye = jnp.eye(sources, dtype=picks.dtype)
    return (picks[:, :, None, :] * eye[:, None, :, None]).reshape(sources * most, sources * tok)


def on_device(grad_out, routes, affinity, saved_hidden, down_proj):
    n_yh = lax.axis_size("yh")
    n_z = lax.axis_size("z")
    exp_devices = n_yh * n_z
    local_experts = down_proj.shape[1]
    expert_count = exp_devices * local_experts
    most = saved_hidden.shape[3]
    width = grad_out.shape[1]
    hidden_units = saved_hidden.shape[4]
    topk = routes.shape[1]
    yh = lax.axis_index("yh")
    z = lax.axis_index("z")
    partner_yh = (yh + 1) % n_yh
    mine = yh * n_z + z
    partner = partner_yh * n_z + z

    totals = jnp.sum(affinity, axis=-1, keepdims=True)
    shares = affinity / totals
    route_weight = (ROUTE_SCALE * shares).astype(jnp.bfloat16)
    slots = local_slots(routes, expert_count)
    meta = jnp.concatenate(
        [
            routes.astype(jnp.bfloat16),
            slots.astype(jnp.bfloat16),
            route_weight,
            jnp.zeros((routes.shape[0], META - 3 * topk), jnp.bfloat16),
        ],
        axis=1,
    )
    carried = jnp.concatenate([grad_out, meta], axis=1)
    gathered = lax.all_gather(carried, "z", axis=0, tiled=False)
    gathered_w = gather_weight(down_proj.reshape(-1, width)).reshape(hidden_units, width)
    gathered, gathered_w = lax.optimization_barrier((gathered, gathered_w))
    meta_all = gathered[:, :, width : width + 3 * topk].astype(jnp.float32)
    route_f = meta_all[:, :, 0:topk]
    slot_f = meta_all[:, :, topk : 2 * topk]
    weight_f = meta_all[:, :, 2 * topk : 3 * topk]

    pick_mine, weight_mine = selection(route_f, slot_f, weight_f, mine, most)
    pick_partner, weight_partner = selection(route_f, slot_f, weight_f, partner, most)
    flat = gathered.reshape(n_z * gathered.shape[1], gathered.shape[2])
    near_rows = jnp.dot(
        block_picks(pick_mine), flat, preferred_element_type=jnp.float32
    ).astype(jnp.bfloat16)[:, :width]
    outgoing = jnp.dot(
        block_picks(pick_partner), flat, preferred_element_type=jnp.float32
    ).astype(jnp.bfloat16)[:, :width]
    swap = [(i, (i + 1) % n_yh) for i in range(n_yh)]
    far_rows = lax.ppermute(outgoing, "yh", perm=swap)
    weight_far = lax.ppermute(weight_partner, "yh", perm=swap)

    hidden = saved_hidden.reshape(exp_devices, most, hidden_units)
    plane = lambda x, p: lax.dynamic_slice_in_dim(x, p * n_z, n_z, axis=0)
    near_hidden = plane(hidden, yh).reshape(n_z * most, hidden_units)
    far_hidden = plane(hidden, partner_yh).reshape(n_z * most, hidden_units)

    def expert_side(rows, row_weight, hid):
        rows = rows.reshape(n_z * most, width)
        scale = row_weight.reshape(n_z * most, 1)
        projected = jnp.einsum(
            "rd,hd->rh", rows, gathered_w, preferred_element_type=jnp.float32
        )
        hidden_grad = (scale * projected).astype(jnp.bfloat16)
        combine = ROUTE_SCALE * jnp.sum(hid.astype(jnp.float32) * projected, axis=-1)
        scaled = (scale * rows.astype(jnp.float32)).astype(jnp.bfloat16)
        term = jnp.einsum("rh,rd->hd", hid, scaled, preferred_element_type=jnp.float32)
        return hidden_grad, combine, term

    near_grad, near_combine, near_term = expert_side(near_rows, weight_mine, near_hidden)
    far_grad, far_combine, far_term = expert_side(far_rows, weight_far, far_hidden)
    grad_term = near_term + far_term
    down_grad = lax.psum_scatter(
        grad_term.astype(jnp.bfloat16), "rep", scatter_dimension=0, tiled=True
    ).astype(jnp.float32)

    first = yh == 0
    hidden_grad = jnp.where(
        first,
        jnp.concatenate([near_grad, far_grad], axis=0),
        jnp.concatenate([far_grad, near_grad], axis=0),
    )
    combine_grad = jnp.where(
        first,
        jnp.concatenate([near_combine, far_combine], axis=0),
        jnp.concatenate([far_combine, near_combine], axis=0),
    ).reshape(exp_devices, most)
    returned = lax.all_to_all(
        combine_grad, ("yh", "z"), split_axis=0, concat_axis=0, tiled=True
    )
    expert_ids = jnp.arange(expert_count, dtype=jnp.int32)
    slot_ids = jnp.arange(most, dtype=jnp.float32)
    by_expert = jnp.sum(
        jnp.where((routes[:, :, None] == expert_ids)[:, :, :, None], returned[None, None], 0.0),
        axis=2,
    )
    route_grad = jnp.sum(
        jnp.where(slots[:, :, None] == slot_ids, by_expert, 0.0), axis=2
    )
    affinity_grad = (route_grad - jnp.sum(route_grad * shares, axis=-1, keepdims=True)) / totals
    return (
        affinity_grad,
        hidden_grad.reshape(saved_hidden.shape),
        down_grad.reshape(down_proj.shape),
    )


def solution(mesh):
    n_exp = mesh.shape["exp"]
    n_yh = 2
    split = Mesh(
        mesh.devices.reshape(mesh.shape["rep"], n_yh, n_exp // n_yh),
        ("rep", "yh", "z"),
    )
    return jax.shard_map(
        on_device,
        mesh=split,
        in_specs=(
            P(TOKENS_SPEC, None),
            P(TOKENS_SPEC, None),
            P(TOKENS_SPEC, None),
            P("rep", ("yh", "z"), None, None, None),
            P("rep", ("yh", "z"), None),
        ),
        out_specs=(
            P(TOKENS_SPEC, None),
            P("rep", ("yh", "z"), None, None, None),
            P("rep", ("yh", "z"), None),
        ),
        check_vma=False,
    )
```

```python
import jax
import jax.numpy as jnp
from jax import lax
from jax.experimental import pallas as pl
from jax.experimental.pallas import tpu as pltpu
from jax.sharding import Mesh
from jax.sharding import PartitionSpec as P

ROUTE_SCALE = 2.5
TOKENS_SPEC = ("rep", "yh", "z")
META = 128
MESH_ID = pl.DeviceIdType.MESH


def gather_weight_kernel(n, w_ref, out_ref, send_sem, recv_sem, fwd_send, fwd_recv, own_sem, local_sem):
    me = lax.axis_index("rep")
    yh = lax.axis_index("yh")
    z = lax.axis_index("z")
    chips = n // 2
    chip = me // 2
    core = me % 2
    partner = chip * 2 + (1 - core)
    barrier = pltpu.get_barrier_semaphore()
    for off in range(1, chips):
        peer = lax.rem(chip + off, chips) * 2 + core
        pl.semaphore_signal(barrier, inc=1, device_id=(peer, yh, z), device_id_type=MESH_ID)
    pl.semaphore_signal(barrier, inc=1, device_id=(partner, yh, z), device_id_type=MESH_ID)
    pl.semaphore_wait(barrier, chips)
    local = pltpu.make_async_copy(w_ref, out_ref.at[me], local_sem)
    local.start()
    own = pltpu.make_async_remote_copy(
        src_ref=w_ref,
        dst_ref=out_ref.at[me],
        send_sem=own_sem.at[0],
        recv_sem=own_sem.at[1],
        device_id=(partner, yh, z),
        device_id_type=MESH_ID,
    )
    own.start()
    sends = []
    for off in range(1, chips):
        peer = lax.rem(chip + off, chips) * 2 + core
        copy = pltpu.make_async_remote_copy(
            src_ref=w_ref,
            dst_ref=out_ref.at[me],
            send_sem=send_sem.at[off],
            recv_sem=recv_sem.at[off],
            device_id=(peer, yh, z),
            device_id_type=MESH_ID,
        )
        copy.start()
        sends.append(copy)
    forwards = []
    for off in range(1, chips):
        source = lax.rem(chip - off + chips, chips) * 2 + core
        incoming = pltpu.make_async_remote_copy(
            src_ref=w_ref,
            dst_ref=out_ref.at[source],
            send_sem=send_sem.at[off],
            recv_sem=recv_sem.at[off],
            device_id=(source, yh, z),
            device_id_type=MESH_ID,
        )
        incoming.wait_recv()
        forward = pltpu.make_async_remote_copy(
            src_ref=out_ref.at[source],
            dst_ref=out_ref.at[source],
            send_sem=fwd_send.at[off],
            recv_sem=fwd_recv.at[off],
            device_id=(partner, yh, z),
            device_id_type=MESH_ID,
        )
        forward.start()
        forwards.append(forward)
    for copy in sends:
        copy.wait_send()
    own.wait_send()
    for forward in forwards:
        forward.wait_send()
    partner_own = pltpu.make_async_remote_copy(
        src_ref=w_ref,
        dst_ref=out_ref.at[partner],
        send_sem=own_sem.at[0],
        recv_sem=own_sem.at[1],
        device_id=(partner, yh, z),
        device_id_type=MESH_ID,
    )
    partner_own.wait_recv()
    for off in range(1, chips):
        source = lax.rem(chip - off + chips, chips) * 2 + (1 - core)
        relayed = pltpu.make_async_remote_copy(
            src_ref=out_ref.at[source],
            dst_ref=out_ref.at[source],
            send_sem=fwd_send.at[off],
            recv_sem=fwd_recv.at[off],
            device_id=(partner, yh, z),
            device_id_type=MESH_ID,
        )
        relayed.wait_recv()
    local.wait()


def gather_weight(w):
    n = lax.axis_size("rep")
    rows, width = w.shape
    return pl.pallas_call(
        lambda *refs: gather_weight_kernel(n, *refs),
        out_shape=jax.ShapeDtypeStruct((n, rows, width), w.dtype),
        in_specs=[pl.BlockSpec(memory_space=pl.ANY)],
        out_specs=pl.BlockSpec(memory_space=pl.ANY),
        scratch_shapes=[
            pltpu.SemaphoreType.DMA((n // 2,)),
            pltpu.SemaphoreType.DMA((n // 2,)),
            pltpu.SemaphoreType.DMA((n // 2,)),
            pltpu.SemaphoreType.DMA((n // 2,)),
            pltpu.SemaphoreType.DMA((2,)),
            pltpu.SemaphoreType.DMA(()),
        ],
        compiler_params=pltpu.CompilerParams(collective_id=0, has_side_effects=True),
        cost_estimate=pl.CostEstimate(
            flops=0, transcendentals=0, bytes_accessed=2 * n * rows * width * w.dtype.itemsize
        ),
    )(w)


def local_slots(routes, expert_count):
    tok = routes.shape[0]
    expert_ids = jnp.arange(expert_count, dtype=jnp.int32)
    hits = routes[:, :, None] == expert_ids
    naming = jnp.sum(hits.astype(jnp.float32), axis=1)
    earlier = (
        jnp.arange(tok, dtype=jnp.int32)[None, :] < jnp.arange(tok, dtype=jnp.int32)[:, None]
    ).astype(jnp.bfloat16)
    before = jnp.dot(earlier, naming.astype(jnp.bfloat16), preferred_element_type=jnp.float32)
    return jnp.sum(jnp.where(hits, before[:, None, :], 0.0), axis=2)


def selection(route_f, slot_f, weight_f, expert, most):
    names = route_f == expert.astype(jnp.float32)
    position = jnp.sum(jnp.where(names, slot_f + 1.0, 0.0), axis=2) - 1.0
    weight = jnp.sum(jnp.where(names, weight_f, 0.0), axis=2)
    picks = position[:, None, :] == jnp.arange(most, dtype=jnp.float32)[None, :, None]
    packed_weight = jnp.sum(jnp.where(picks, weight[:, None, :], 0.0), axis=2)
    return picks.astype(jnp.bfloat16), packed_weight


def block_picks(picks):
    sources, most, tok = picks.shape
    eye = jnp.eye(sources, dtype=picks.dtype)
    return (picks[:, :, None, :] * eye[:, None, :, None]).reshape(sources * most, sources * tok)


def on_device(grad_out, routes, affinity, saved_hidden, down_proj):
    n_yh = lax.axis_size("yh")
    n_z = lax.axis_size("z")
    exp_devices = n_yh * n_z
    local_experts = down_proj.shape[1]
    expert_count = exp_devices * local_experts
    most = saved_hidden.shape[3]
    width = grad_out.shape[1]
    hidden_units = saved_hidden.shape[4]
    topk = routes.shape[1]
    tok = routes.shape[0]
    yh = lax.axis_index("yh")
    z = lax.axis_index("z")
    partner_yh = (yh + 1) % n_yh
    mine = yh * n_z + z
    partner = partner_yh * n_z + z

    totals = jnp.sum(affinity, axis=-1, keepdims=True)
    shares = affinity / totals
    route_weight = (ROUTE_SCALE * shares).astype(jnp.bfloat16)
    slots = local_slots(routes, expert_count)
    meta = jnp.concatenate(
        [
            routes.astype(jnp.bfloat16),
            slots.astype(jnp.bfloat16),
            route_weight,
            jnp.zeros((routes.shape[0], META - 3 * topk), jnp.bfloat16),
        ],
        axis=1,
    )
    half = width // 2
    swap = [(i, (i + 1) % n_yh) for i in range(n_yh)]
    first_part = jnp.concatenate([grad_out[:, :half], meta], axis=1)
    gathered_a = lax.all_gather(first_part, "z", axis=0, tiled=True)
    gathered_w = gather_weight(down_proj.reshape(-1, width)).reshape(hidden_units, width)
    gathered_a, gathered_w = lax.optimization_barrier((gathered_a, gathered_w))
    meta_all = gathered_a[:, half : half + 3 * topk].astype(jnp.float32).reshape(n_z, tok, 3 * topk)
    route_f = meta_all[:, :, 0:topk]
    slot_f = meta_all[:, :, topk : 2 * topk]
    weight_f = meta_all[:, :, 2 * topk : 3 * topk]

    pick_mine, weight_mine = selection(route_f, slot_f, weight_f, mine, most)
    pick_partner, weight_partner = selection(route_f, slot_f, weight_f, partner, most)
    pick_mine = block_picks(pick_mine)
    pick_partner = block_picks(pick_partner)
    weight_far = lax.ppermute(weight_partner, "yh", perm=swap)

    def pack(gathered):
        out = jnp.dot(pick_partner, gathered, preferred_element_type=jnp.float32)
        far = lax.ppermute(out.astype(jnp.bfloat16), "yh", perm=swap)
        near = jnp.dot(pick_mine, gathered, preferred_element_type=jnp.float32)
        return near.astype(jnp.bfloat16), far

    near_a, far_a = pack(gathered_a[:, :half])
    second_part, _ = lax.optimization_barrier((grad_out[:, half:], gathered_a))
    gathered_b = lax.all_gather(second_part, "z", axis=0, tiled=True)
    near_b, far_b = pack(gathered_b)
    near_rows = jnp.concatenate([near_a, near_b], axis=1)
    far_rows = jnp.concatenate([far_a, far_b], axis=1)

    hidden = saved_hidden.reshape(exp_devices, most, hidden_units)
    plane = lambda x, p: lax.dynamic_slice_in_dim(x, p * n_z, n_z, axis=0)
    near_hidden = plane(hidden, yh).reshape(n_z * most, hidden_units)
    far_hidden = plane(hidden, partner_yh).reshape(n_z * most, hidden_units)

    def expert_side(rows, row_weight, hid):
        rows = rows.reshape(n_z * most, width)
        scale = row_weight.reshape(n_z * most, 1)
        projected = jnp.einsum(
            "rd,hd->rh", rows, gathered_w, preferred_element_type=jnp.float32
        )
        hidden_grad = (scale * projected).astype(jnp.bfloat16)
        combine = ROUTE_SCALE * jnp.sum(hid.astype(jnp.float32) * projected, axis=-1)
        scaled = (scale * rows.astype(jnp.float32)).astype(jnp.bfloat16)
        term = jnp.einsum("rh,rd->hd", hid, scaled, preferred_element_type=jnp.float32)
        return hidden_grad, combine, term

    near_grad, near_combine, near_term = expert_side(near_rows, weight_mine, near_hidden)
    far_grad, far_combine, far_term = expert_side(far_rows, weight_far, far_hidden)
    grad_term = near_term + far_term
    down_grad = lax.psum_scatter(
        grad_term.astype(jnp.bfloat16), "rep", scatter_dimension=0, tiled=True
    ).astype(jnp.float32)

    first = yh == 0
    hidden_grad = jnp.where(
        first,
        jnp.concatenate([near_grad, far_grad], axis=0),
        jnp.concatenate([far_grad, near_grad], axis=0),
    )
    combine_grad = jnp.where(
        first,
        jnp.concatenate([near_combine, far_combine], axis=0),
        jnp.concatenate([far_combine, near_combine], axis=0),
    ).reshape(exp_devices, most)
    returned = lax.all_to_all(
        combine_grad, ("yh", "z"), split_axis=0, concat_axis=0, tiled=True
    )
    expert_ids = jnp.arange(expert_count, dtype=jnp.int32)
    slot_ids = jnp.arange(most, dtype=jnp.float32)
    by_expert = jnp.sum(
        jnp.where((routes[:, :, None] == expert_ids)[:, :, :, None], returned[None, None], 0.0),
        axis=2,
    )
    route_grad = jnp.sum(
        jnp.where(slots[:, :, None] == slot_ids, by_expert, 0.0), axis=2
    )
    affinity_grad = (route_grad - jnp.sum(route_grad * shares, axis=-1, keepdims=True)) / totals
    return (
        affinity_grad,
        hidden_grad.reshape(saved_hidden.shape),
        down_grad.reshape(down_proj.shape),
    )


def solution(mesh):
    n_exp = mesh.shape["exp"]
    n_yh = 2
    split = Mesh(
        mesh.devices.reshape(mesh.shape["rep"], n_yh, n_exp // n_yh),
        ("rep", "yh", "z"),
    )
    return jax.shard_map(
        on_device,
        mesh=split,
        in_specs=(
            P(TOKENS_SPEC, None),
            P(TOKENS_SPEC, None),
            P(TOKENS_SPEC, None),
            P("rep", ("yh", "z"), None, None, None),
            P("rep", ("yh", "z"), None),
        ),
        out_specs=(
            P(TOKENS_SPEC, None),
            P("rep", ("yh", "z"), None, None, None),
            P("rep", ("yh", "z"), None),
        ),
        check_vma=False,
    )
```

```python
import jax
import jax.numpy as jnp
from jax import lax
from jax.experimental import pallas as pl
from jax.experimental.pallas import tpu as pltpu
from jax.sharding import Mesh
from jax.sharding import PartitionSpec as P

ROUTE_SCALE = 2.5
TOKENS_SPEC = ("rep", "yh", "z")
META = 128
MESH_ID = pl.DeviceIdType.MESH


def gather_weight_kernel(n, w_ref, out_ref, send_sem, recv_sem, fwd_send, fwd_recv, own_sem, local_sem):
    me = lax.axis_index("rep")
    yh = lax.axis_index("yh")
    z = lax.axis_index("z")
    chips = n // 2
    chip = me // 2
    core = me % 2
    partner = chip * 2 + (1 - core)
    barrier = pltpu.get_barrier_semaphore()
    for off in range(1, chips):
        peer = lax.rem(chip + off, chips) * 2 + core
        pl.semaphore_signal(barrier, inc=1, device_id=(peer, yh, z), device_id_type=MESH_ID)
    pl.semaphore_signal(barrier, inc=1, device_id=(partner, yh, z), device_id_type=MESH_ID)
    pl.semaphore_wait(barrier, chips)
    local = pltpu.make_async_copy(w_ref, out_ref.at[me], local_sem)
    local.start()
    own = pltpu.make_async_remote_copy(
        src_ref=w_ref,
        dst_ref=out_ref.at[me],
        send_sem=own_sem.at[0],
        recv_sem=own_sem.at[1],
        device_id=(partner, yh, z),
        device_id_type=MESH_ID,
    )
    own.start()
    sends = []
    for off in range(1, chips):
        peer = lax.rem(chip + off, chips) * 2 + core
        copy = pltpu.make_async_remote_copy(
            src_ref=w_ref,
            dst_ref=out_ref.at[me],
            send_sem=send_sem.at[off],
            recv_sem=recv_sem.at[off],
            device_id=(peer, yh, z),
            device_id_type=MESH_ID,
        )
        copy.start()
        sends.append(copy)
    forwards = []
    for off in range(1, chips):
        source = lax.rem(chip - off + chips, chips) * 2 + core
        incoming = pltpu.make_async_remote_copy(
            src_ref=w_ref,
            dst_ref=out_ref.at[source],
            send_sem=send_sem.at[off],
            recv_sem=recv_sem.at[off],
            device_id=(source, yh, z),
            device_id_type=MESH_ID,
        )
        incoming.wait_recv()
        forward = pltpu.make_async_remote_copy(
            src_ref=out_ref.at[source],
            dst_ref=out_ref.at[source],
            send_sem=fwd_send.at[off],
            recv_sem=fwd_recv.at[off],
            device_id=(partner, yh, z),
            device_id_type=MESH_ID,
        )
        forward.start()
        forwards.append(forward)
    for copy in sends:
        copy.wait_send()
    own.wait_send()
    for forward in forwards:
        forward.wait_send()
    partner_own = pltpu.make_async_remote_copy(
        src_ref=w_ref,
        dst_ref=out_ref.at[partner],
        send_sem=own_sem.at[0],
        recv_sem=own_sem.at[1],
        device_id=(partner, yh, z),
        device_id_type=MESH_ID,
    )
    partner_own.wait_recv()
    for off in range(1, chips):
        source = lax.rem(chip - off + chips, chips) * 2 + (1 - core)
        relayed = pltpu.make_async_remote_copy(
            src_ref=out_ref.at[source],
            dst_ref=out_ref.at[source],
            send_sem=fwd_send.at[off],
            recv_sem=fwd_recv.at[off],
            device_id=(partner, yh, z),
            device_id_type=MESH_ID,
        )
        relayed.wait_recv()
    local.wait()


def gather_weight(w):
    n = lax.axis_size("rep")
    rows, width = w.shape
    return pl.pallas_call(
        lambda *refs: gather_weight_kernel(n, *refs),
        out_shape=jax.ShapeDtypeStruct((n, rows, width), w.dtype),
        in_specs=[pl.BlockSpec(memory_space=pl.ANY)],
        out_specs=pl.BlockSpec(memory_space=pl.ANY),
        scratch_shapes=[
            pltpu.SemaphoreType.DMA((n // 2,)),
            pltpu.SemaphoreType.DMA((n // 2,)),
            pltpu.SemaphoreType.DMA((n // 2,)),
            pltpu.SemaphoreType.DMA((n // 2,)),
            pltpu.SemaphoreType.DMA((2,)),
            pltpu.SemaphoreType.DMA(()),
        ],
        compiler_params=pltpu.CompilerParams(collective_id=0, has_side_effects=True),
        cost_estimate=pl.CostEstimate(
            flops=0, transcendentals=0, bytes_accessed=2 * n * rows * width * w.dtype.itemsize
        ),
    )(w)


def local_slots(routes, expert_count):
    tok = routes.shape[0]
    expert_ids = jnp.arange(expert_count, dtype=jnp.int32)
    hits = routes[:, :, None] == expert_ids
    naming = jnp.sum(hits.astype(jnp.float32), axis=1)
    earlier = (
        jnp.arange(tok, dtype=jnp.int32)[None, :] < jnp.arange(tok, dtype=jnp.int32)[:, None]
    ).astype(jnp.bfloat16)
    before = jnp.dot(earlier, naming.astype(jnp.bfloat16), preferred_element_type=jnp.float32)
    return jnp.sum(jnp.where(hits, before[:, None, :], 0.0), axis=2)


def selection(route_f, slot_f, weight_f, expert, most):
    names = route_f == expert.astype(jnp.float32)
    position = jnp.sum(jnp.where(names, slot_f + 1.0, 0.0), axis=2) - 1.0
    weight = jnp.sum(jnp.where(names, weight_f, 0.0), axis=2)
    picks = position[:, None, :] == jnp.arange(most, dtype=jnp.float32)[None, :, None]
    packed_weight = jnp.sum(jnp.where(picks, weight[:, None, :], 0.0), axis=2)
    return picks.astype(jnp.bfloat16), packed_weight


def block_picks(picks):
    sources, most, tok = picks.shape
    eye = jnp.eye(sources, dtype=picks.dtype)
    return (picks[:, :, None, :] * eye[:, None, :, None]).reshape(sources * most, sources * tok)


def on_device(grad_out, routes, affinity, saved_hidden, down_proj):
    n_yh = lax.axis_size("yh")
    n_z = lax.axis_size("z")
    exp_devices = n_yh * n_z
    local_experts = down_proj.shape[1]
    expert_count = exp_devices * local_experts
    most = saved_hidden.shape[3]
    width = grad_out.shape[1]
    hidden_units = saved_hidden.shape[4]
    topk = routes.shape[1]
    tok = routes.shape[0]
    yh = lax.axis_index("yh")
    z = lax.axis_index("z")
    partner_yh = (yh + 1) % n_yh
    mine = yh * n_z + z
    partner = partner_yh * n_z + z

    totals = jnp.sum(affinity, axis=-1, keepdims=True)
    shares = affinity / totals
    route_weight = (ROUTE_SCALE * shares).astype(jnp.bfloat16)
    slots = local_slots(routes, expert_count)
    meta = jnp.concatenate(
        [
            routes.astype(jnp.bfloat16),
            slots.astype(jnp.bfloat16),
            route_weight,
            jnp.zeros((routes.shape[0], META - 3 * topk), jnp.bfloat16),
        ],
        axis=1,
    )
    half = (width // 128 * 9 // 14) * 128
    swap = [(i, (i + 1) % n_yh) for i in range(n_yh)]
    first_part = jnp.concatenate([grad_out[:, :half], meta], axis=1)
    gathered_a = lax.all_gather(first_part, "z", axis=0, tiled=True)
    gathered_w = gather_weight(down_proj.reshape(-1, width)).reshape(hidden_units, width)
    gathered_a, gathered_w = lax.optimization_barrier((gathered_a, gathered_w))
    meta_all = gathered_a[:, half : half + 3 * topk].astype(jnp.float32).reshape(n_z, tok, 3 * topk)
    route_f = meta_all[:, :, 0:topk]
    slot_f = meta_all[:, :, topk : 2 * topk]
    weight_f = meta_all[:, :, 2 * topk : 3 * topk]

    pick_mine, weight_mine = selection(route_f, slot_f, weight_f, mine, most)
    pick_partner, weight_partner = selection(route_f, slot_f, weight_f, partner, most)
    pick_mine = block_picks(pick_mine)
    pick_partner = block_picks(pick_partner)
    weight_far = lax.ppermute(weight_partner, "yh", perm=swap)

    def pack(gathered):
        out = jnp.dot(pick_partner, gathered, preferred_element_type=jnp.float32)
        far = lax.ppermute(out.astype(jnp.bfloat16), "yh", perm=swap)
        near = jnp.dot(pick_mine, gathered, preferred_element_type=jnp.float32)
        return near.astype(jnp.bfloat16), far

    near_a, far_a = pack(gathered_a[:, :half])
    second_part, _ = lax.optimization_barrier((grad_out[:, half:], gathered_a))
    gathered_b = lax.all_gather(second_part, "z", axis=0, tiled=True)
    near_b, far_b = pack(gathered_b)
    near_rows = jnp.concatenate([near_a, near_b], axis=1)
    far_rows = jnp.concatenate([far_a, far_b], axis=1)

    hidden = saved_hidden.reshape(exp_devices, most, hidden_units)
    plane = lambda x, p: lax.dynamic_slice_in_dim(x, p * n_z, n_z, axis=0)
    near_hidden = plane(hidden, yh).reshape(n_z * most, hidden_units)
    far_hidden = plane(hidden, partner_yh).reshape(n_z * most, hidden_units)

    def expert_side(rows, row_weight, hid):
        rows = rows.reshape(n_z * most, width)
        scale = row_weight.reshape(n_z * most, 1)
        projected = jnp.einsum(
            "rd,hd->rh", rows, gathered_w, preferred_element_type=jnp.float32
        )
        hidden_grad = (scale * projected).astype(jnp.bfloat16)
        combine = ROUTE_SCALE * jnp.sum(hid.astype(jnp.float32) * projected, axis=-1)
        scaled = (scale * rows.astype(jnp.float32)).astype(jnp.bfloat16)
        term = jnp.einsum("rh,rd->hd", hid, scaled, preferred_element_type=jnp.float32)
        return hidden_grad, combine, term

    near_grad, near_combine, near_term = expert_side(near_rows, weight_mine, near_hidden)
    far_grad, far_combine, far_term = expert_side(far_rows, weight_far, far_hidden)
    grad_term = near_term + far_term
    down_grad = lax.psum_scatter(
        grad_term.astype(jnp.bfloat16), "rep", scatter_dimension=0, tiled=True
    ).astype(jnp.float32)

    first = yh == 0
    hidden_grad = jnp.where(
        first,
        jnp.concatenate([near_grad, far_grad], axis=0),
        jnp.concatenate([far_grad, near_grad], axis=0),
    )
    combine_grad = jnp.where(
        first,
        jnp.concatenate([near_combine, far_combine], axis=0),
        jnp.concatenate([far_combine, near_combine], axis=0),
    ).reshape(exp_devices, most)
    returned = lax.all_to_all(
        combine_grad, ("yh", "z"), split_axis=0, concat_axis=0, tiled=True
    )
    expert_ids = jnp.arange(expert_count, dtype=jnp.int32)
    slot_ids = jnp.arange(most, dtype=jnp.float32)
    by_expert = jnp.sum(
        jnp.where((routes[:, :, None] == expert_ids)[:, :, :, None], returned[None, None], 0.0),
        axis=2,
    )
    route_grad = jnp.sum(
        jnp.where(slots[:, :, None] == slot_ids, by_expert, 0.0), axis=2
    )
    affinity_grad = (route_grad - jnp.sum(route_grad * shares, axis=-1, keepdims=True)) / totals
    return (
        affinity_grad,
        hidden_grad.reshape(saved_hidden.shape),
        down_grad.reshape(down_proj.shape),
    )


def solution(mesh):
    n_exp = mesh.shape["exp"]
    n_yh = 2
    split = Mesh(
        mesh.devices.reshape(mesh.shape["rep"], n_yh, n_exp // n_yh),
        ("rep", "yh", "z"),
    )
    return jax.shard_map(
        on_device,
        mesh=split,
        in_specs=(
            P(TOKENS_SPEC, None),
            P(TOKENS_SPEC, None),
            P(TOKENS_SPEC, None),
            P("rep", ("yh", "z"), None, None, None),
            P("rep", ("yh", "z"), None),
        ),
        out_specs=(
            P(TOKENS_SPEC, None),
            P("rep", ("yh", "z"), None, None, None),
            P("rep", ("yh", "z"), None),
        ),
        check_vma=False,
    )
```

```python
import jax
import jax.numpy as jnp
from jax import lax
from jax.experimental import pallas as pl
from jax.experimental.pallas import tpu as pltpu
from jax.sharding import Mesh
from jax.sharding import PartitionSpec as P

ROUTE_SCALE = 2.5
TOKENS_SPEC = ("rc", "core", "yh", "z")
REP = ("rc", "core")
META = 128
MESH_ID = pl.DeviceIdType.MESH


def gather_weight_kernel(n, w_ref, out_ref, send_sem, recv_sem, fwd_send, fwd_recv, own_sem, local_sem):
    chip = lax.axis_index("rc")
    core = lax.axis_index("core")
    yh = lax.axis_index("yh")
    z = lax.axis_index("z")
    chips = n // 2
    me = chip * 2 + core
    partner = chip * 2 + (1 - core)
    barrier = pltpu.get_barrier_semaphore()
    for off in range(1, chips):
        peer = lax.rem(chip + off, chips) * 2 + core
        pl.semaphore_signal(barrier, inc=1, device_id=(peer // 2, peer % 2, yh, z), device_id_type=MESH_ID)
    pl.semaphore_signal(barrier, inc=1, device_id=(partner // 2, partner % 2, yh, z), device_id_type=MESH_ID)
    pl.semaphore_wait(barrier, chips)
    local = pltpu.make_async_copy(w_ref, out_ref.at[me], local_sem)
    local.start()
    own = pltpu.make_async_remote_copy(
        src_ref=w_ref,
        dst_ref=out_ref.at[me],
        send_sem=own_sem.at[0],
        recv_sem=own_sem.at[1],
        device_id=(partner // 2, partner % 2, yh, z),
        device_id_type=MESH_ID,
    )
    own.start()
    sends = []
    for off in range(1, chips):
        peer = lax.rem(chip + off, chips) * 2 + core
        copy = pltpu.make_async_remote_copy(
            src_ref=w_ref,
            dst_ref=out_ref.at[me],
            send_sem=send_sem.at[off],
            recv_sem=recv_sem.at[off],
            device_id=(peer // 2, peer % 2, yh, z),
            device_id_type=MESH_ID,
        )
        copy.start()
        sends.append(copy)
    forwards = []
    for off in range(1, chips):
        source = lax.rem(chip - off + chips, chips) * 2 + core
        incoming = pltpu.make_async_remote_copy(
            src_ref=w_ref,
            dst_ref=out_ref.at[source],
            send_sem=send_sem.at[off],
            recv_sem=recv_sem.at[off],
            device_id=(source // 2, source % 2, yh, z),
            device_id_type=MESH_ID,
        )
        incoming.wait_recv()
        forward = pltpu.make_async_remote_copy(
            src_ref=out_ref.at[source],
            dst_ref=out_ref.at[source],
            send_sem=fwd_send.at[off],
            recv_sem=fwd_recv.at[off],
            device_id=(partner // 2, partner % 2, yh, z),
            device_id_type=MESH_ID,
        )
        forward.start()
        forwards.append(forward)
    for copy in sends:
        copy.wait_send()
    own.wait_send()
    for forward in forwards:
        forward.wait_send()
    partner_own = pltpu.make_async_remote_copy(
        src_ref=w_ref,
        dst_ref=out_ref.at[partner],
        send_sem=own_sem.at[0],
        recv_sem=own_sem.at[1],
        device_id=(partner // 2, partner % 2, yh, z),
        device_id_type=MESH_ID,
    )
    partner_own.wait_recv()
    for off in range(1, chips):
        source = lax.rem(chip - off + chips, chips) * 2 + (1 - core)
        relayed = pltpu.make_async_remote_copy(
            src_ref=out_ref.at[source],
            dst_ref=out_ref.at[source],
            send_sem=fwd_send.at[off],
            recv_sem=fwd_recv.at[off],
            device_id=(partner // 2, partner % 2, yh, z),
            device_id_type=MESH_ID,
        )
        relayed.wait_recv()
    local.wait()


def gather_weight(w):
    n = lax.axis_size("rc") * lax.axis_size("core")
    rows, width = w.shape
    return pl.pallas_call(
        lambda *refs: gather_weight_kernel(n, *refs),
        out_shape=jax.ShapeDtypeStruct((n, rows, width), w.dtype),
        in_specs=[pl.BlockSpec(memory_space=pl.ANY)],
        out_specs=pl.BlockSpec(memory_space=pl.ANY),
        scratch_shapes=[
            pltpu.SemaphoreType.DMA((n // 2,)),
            pltpu.SemaphoreType.DMA((n // 2,)),
            pltpu.SemaphoreType.DMA((n // 2,)),
            pltpu.SemaphoreType.DMA((n // 2,)),
            pltpu.SemaphoreType.DMA((2,)),
            pltpu.SemaphoreType.DMA(()),
        ],
        compiler_params=pltpu.CompilerParams(collective_id=0, has_side_effects=True),
        cost_estimate=pl.CostEstimate(
            flops=0, transcendentals=0, bytes_accessed=2 * n * rows * width * w.dtype.itemsize
        ),
    )(w)


def local_slots(routes, expert_count):
    tok = routes.shape[0]
    expert_ids = jnp.arange(expert_count, dtype=jnp.int32)
    hits = routes[:, :, None] == expert_ids
    naming = jnp.sum(hits.astype(jnp.float32), axis=1)
    earlier = (
        jnp.arange(tok, dtype=jnp.int32)[None, :] < jnp.arange(tok, dtype=jnp.int32)[:, None]
    ).astype(jnp.bfloat16)
    before = jnp.dot(earlier, naming.astype(jnp.bfloat16), preferred_element_type=jnp.float32)
    return jnp.sum(jnp.where(hits, before[:, None, :], 0.0), axis=2)


def selection(route_f, slot_f, weight_f, expert, most):
    names = route_f == expert.astype(jnp.float32)
    position = jnp.sum(jnp.where(names, slot_f + 1.0, 0.0), axis=2) - 1.0
    weight = jnp.sum(jnp.where(names, weight_f, 0.0), axis=2)
    picks = position[:, None, :] == jnp.arange(most, dtype=jnp.float32)[None, :, None]
    packed_weight = jnp.sum(jnp.where(picks, weight[:, None, :], 0.0), axis=2)
    return picks.astype(jnp.bfloat16), packed_weight


def block_picks(picks):
    sources, most, tok = picks.shape
    eye = jnp.eye(sources, dtype=picks.dtype)
    return (picks[:, :, None, :] * eye[:, None, :, None]).reshape(sources * most, sources * tok)


def on_device(grad_out, routes, affinity, saved_hidden, down_proj):
    n_yh = lax.axis_size("yh")
    n_z = lax.axis_size("z")
    exp_devices = n_yh * n_z
    local_experts = down_proj.shape[1]
    expert_count = exp_devices * local_experts
    most = saved_hidden.shape[3]
    width = grad_out.shape[1]
    hidden_units = saved_hidden.shape[4]
    topk = routes.shape[1]
    tok = routes.shape[0]
    yh = lax.axis_index("yh")
    z = lax.axis_index("z")
    partner_yh = (yh + 1) % n_yh
    mine = yh * n_z + z
    partner = partner_yh * n_z + z

    totals = jnp.sum(affinity, axis=-1, keepdims=True)
    shares = affinity / totals
    route_weight = (ROUTE_SCALE * shares).astype(jnp.bfloat16)
    slots = local_slots(routes, expert_count)
    meta = jnp.concatenate(
        [
            routes.astype(jnp.bfloat16),
            slots.astype(jnp.bfloat16),
            route_weight,
            jnp.zeros((routes.shape[0], META - 3 * topk), jnp.bfloat16),
        ],
        axis=1,
    )
    half = width // 2
    swap = [(i, (i + 1) % n_yh) for i in range(n_yh)]
    first_part = jnp.concatenate([grad_out[:, :half], meta], axis=1)
    gathered_a = lax.all_gather(first_part, "z", axis=0, tiled=True)
    gathered_w = gather_weight(down_proj.reshape(-1, width)).reshape(hidden_units, width)
    gathered_a, gathered_w = lax.optimization_barrier((gathered_a, gathered_w))
    meta_all = gathered_a[:, half : half + 3 * topk].astype(jnp.float32).reshape(n_z, tok, 3 * topk)
    route_f = meta_all[:, :, 0:topk]
    slot_f = meta_all[:, :, topk : 2 * topk]
    weight_f = meta_all[:, :, 2 * topk : 3 * topk]

    pick_mine, weight_mine = selection(route_f, slot_f, weight_f, mine, most)
    pick_partner, weight_partner = selection(route_f, slot_f, weight_f, partner, most)
    pick_mine = block_picks(pick_mine)
    pick_partner = block_picks(pick_partner)
    weight_far = lax.ppermute(weight_partner, "yh", perm=swap)

    def pack(gathered):
        out = jnp.dot(pick_partner, gathered, preferred_element_type=jnp.float32)
        far = lax.ppermute(out.astype(jnp.bfloat16), "yh", perm=swap)
        near = jnp.dot(pick_mine, gathered, preferred_element_type=jnp.float32)
        return near.astype(jnp.bfloat16), far

    near_a, far_a = pack(gathered_a[:, :half])
    second_part, _ = lax.optimization_barrier((grad_out[:, half:], gathered_a))
    gathered_b = lax.all_gather(second_part, "z", axis=0, tiled=True)
    near_b, far_b = pack(gathered_b)
    near_rows = jnp.concatenate([near_a, near_b], axis=1)
    far_rows = jnp.concatenate([far_a, far_b], axis=1)

    hidden = saved_hidden.reshape(exp_devices, most, hidden_units)
    plane = lambda x, p: lax.dynamic_slice_in_dim(x, p * n_z, n_z, axis=0)
    near_hidden = plane(hidden, yh).reshape(n_z * most, hidden_units)
    far_hidden = plane(hidden, partner_yh).reshape(n_z * most, hidden_units)

    def expert_side(rows, row_weight, hid):
        rows = rows.reshape(n_z * most, width)
        scale = row_weight.reshape(n_z * most, 1)
        projected = jnp.einsum(
            "rd,hd->rh", rows, gathered_w, preferred_element_type=jnp.float32
        )
        hidden_grad = (scale * projected).astype(jnp.bfloat16)
        combine = ROUTE_SCALE * jnp.sum(hid.astype(jnp.float32) * projected, axis=-1)
        scaled = (scale * rows.astype(jnp.float32)).astype(jnp.bfloat16)
        term = jnp.einsum("rh,rd->hd", hid, scaled, preferred_element_type=jnp.float32)
        return hidden_grad, combine, term

    near_grad, near_combine, near_term = expert_side(near_rows, weight_mine, near_hidden)
    far_grad, far_combine, far_term = expert_side(far_rows, weight_far, far_hidden)
    grad_term = near_term + far_term
    n_rc = lax.axis_size("rc")
    n_core = lax.axis_size("core")
    by_core = jnp.swapaxes(
        grad_term.astype(jnp.bfloat16).reshape(n_rc, n_core, -1, width), 0, 1
    )
    on_chip = lax.psum_scatter(by_core, "core", scatter_dimension=0, tiled=True)
    down_grad = lax.psum_scatter(
        on_chip.reshape(n_rc, -1, width), "rc", scatter_dimension=0, tiled=True
    ).astype(jnp.float32)

    first = yh == 0
    hidden_grad = jnp.where(
        first,
        jnp.concatenate([near_grad, far_grad], axis=0),
        jnp.concatenate([far_grad, near_grad], axis=0),
    )
    combine_grad = jnp.where(
        first,
        jnp.concatenate([near_combine, far_combine], axis=0),
        jnp.concatenate([far_combine, near_combine], axis=0),
    ).reshape(exp_devices, most)
    returned = lax.all_to_all(
        combine_grad, ("yh", "z"), split_axis=0, concat_axis=0, tiled=True
    )
    expert_ids = jnp.arange(expert_count, dtype=jnp.int32)
    slot_ids = jnp.arange(most, dtype=jnp.float32)
    by_expert = jnp.sum(
        jnp.where((routes[:, :, None] == expert_ids)[:, :, :, None], returned[None, None], 0.0),
        axis=2,
    )
    route_grad = jnp.sum(
        jnp.where(slots[:, :, None] == slot_ids, by_expert, 0.0), axis=2
    )
    affinity_grad = (route_grad - jnp.sum(route_grad * shares, axis=-1, keepdims=True)) / totals
    return (
        affinity_grad,
        hidden_grad.reshape(saved_hidden.shape),
        down_grad.reshape(down_proj.shape),
    )


def solution(mesh):
    n_exp = mesh.shape["exp"]
    n_yh = 2
    n_rep = mesh.shape["rep"]
    split = Mesh(
        mesh.devices.reshape(n_rep // 2, 2, n_yh, n_exp // n_yh),
        ("rc", "core", "yh", "z"),
    )
    return jax.shard_map(
        on_device,
        mesh=split,
        in_specs=(
            P(TOKENS_SPEC, None),
            P(TOKENS_SPEC, None),
            P(TOKENS_SPEC, None),
            P(REP, ("yh", "z"), None, None, None),
            P(REP, ("yh", "z"), None),
        ),
        out_specs=(
            P(TOKENS_SPEC, None),
            P(REP, ("yh", "z"), None, None, None),
            P(REP, ("yh", "z"), None),
        ),
        check_vma=False,
    )
```

```python
import jax
import jax.numpy as jnp
from jax import lax
from jax.experimental import pallas as pl
from jax.experimental.pallas import tpu as pltpu
from jax.sharding import Mesh
from jax.sharding import PartitionSpec as P

ROUTE_SCALE = 2.5
TOKENS_SPEC = ("rc", "core", "yh", "z")
REP = ("rc", "core")
META = 128
MESH_ID = pl.DeviceIdType.MESH


def gather_weight_kernel(n, w_ref, out_ref, send_sem, recv_sem, fwd_send, fwd_recv, own_sem, local_sem):
    chip = lax.axis_index("rc")
    core = lax.axis_index("core")
    yh = lax.axis_index("yh")
    z = lax.axis_index("z")
    chips = n // 2
    me = chip * 2 + core
    partner = chip * 2 + (1 - core)
    barrier = pltpu.get_barrier_semaphore()
    for off in range(1, chips):
        peer = lax.rem(chip + off, chips) * 2 + core
        pl.semaphore_signal(barrier, inc=1, device_id=(peer // 2, peer % 2, yh, z), device_id_type=MESH_ID)
    pl.semaphore_signal(barrier, inc=1, device_id=(partner // 2, partner % 2, yh, z), device_id_type=MESH_ID)
    pl.semaphore_wait(barrier, chips)
    local = pltpu.make_async_copy(w_ref, out_ref.at[me], local_sem)
    local.start()
    own = pltpu.make_async_remote_copy(
        src_ref=w_ref,
        dst_ref=out_ref.at[me],
        send_sem=own_sem.at[0],
        recv_sem=own_sem.at[1],
        device_id=(partner // 2, partner % 2, yh, z),
        device_id_type=MESH_ID,
    )
    own.start()
    sends = []
    for off in range(1, chips):
        peer = lax.rem(chip + off, chips) * 2 + core
        copy = pltpu.make_async_remote_copy(
            src_ref=w_ref,
            dst_ref=out_ref.at[me],
            send_sem=send_sem.at[off],
            recv_sem=recv_sem.at[off],
            device_id=(peer // 2, peer % 2, yh, z),
            device_id_type=MESH_ID,
        )
        copy.start()
        sends.append(copy)
    forwards = []
    for off in range(1, chips):
        source = lax.rem(chip - off + chips, chips) * 2 + core
        incoming = pltpu.make_async_remote_copy(
            src_ref=w_ref,
            dst_ref=out_ref.at[source],
            send_sem=send_sem.at[off],
            recv_sem=recv_sem.at[off],
            device_id=(source // 2, source % 2, yh, z),
            device_id_type=MESH_ID,
        )
        incoming.wait_recv()
        forward = pltpu.make_async_remote_copy(
            src_ref=out_ref.at[source],
            dst_ref=out_ref.at[source],
            send_sem=fwd_send.at[off],
            recv_sem=fwd_recv.at[off],
            device_id=(partner // 2, partner % 2, yh, z),
            device_id_type=MESH_ID,
        )
        forward.start()
        forwards.append(forward)
    for copy in sends:
        copy.wait_send()
    own.wait_send()
    for forward in forwards:
        forward.wait_send()
    partner_own = pltpu.make_async_remote_copy(
        src_ref=w_ref,
        dst_ref=out_ref.at[partner],
        send_sem=own_sem.at[0],
        recv_sem=own_sem.at[1],
        device_id=(partner // 2, partner % 2, yh, z),
        device_id_type=MESH_ID,
    )
    partner_own.wait_recv()
    for off in range(1, chips):
        source = lax.rem(chip - off + chips, chips) * 2 + (1 - core)
        relayed = pltpu.make_async_remote_copy(
            src_ref=out_ref.at[source],
            dst_ref=out_ref.at[source],
            send_sem=fwd_send.at[off],
            recv_sem=fwd_recv.at[off],
            device_id=(partner // 2, partner % 2, yh, z),
            device_id_type=MESH_ID,
        )
        relayed.wait_recv()
    local.wait()


def gather_weight(w):
    n = lax.axis_size("rc") * lax.axis_size("core")
    rows, width = w.shape
    return pl.pallas_call(
        lambda *refs: gather_weight_kernel(n, *refs),
        out_shape=jax.ShapeDtypeStruct((n, rows, width), w.dtype),
        in_specs=[pl.BlockSpec(memory_space=pl.ANY)],
        out_specs=pl.BlockSpec(memory_space=pl.ANY),
        scratch_shapes=[
            pltpu.SemaphoreType.DMA((n // 2,)),
            pltpu.SemaphoreType.DMA((n // 2,)),
            pltpu.SemaphoreType.DMA((n // 2,)),
            pltpu.SemaphoreType.DMA((n // 2,)),
            pltpu.SemaphoreType.DMA((2,)),
            pltpu.SemaphoreType.DMA(()),
        ],
        compiler_params=pltpu.CompilerParams(collective_id=0, has_side_effects=True),
        cost_estimate=pl.CostEstimate(
            flops=0, transcendentals=0, bytes_accessed=2 * n * rows * width * w.dtype.itemsize
        ),
    )(w)


def partner_kernel(x_ref, out_ref, sems):
    chip = lax.axis_index("rc")
    core = lax.axis_index("core")
    yh = lax.axis_index("yh")
    z = lax.axis_index("z")
    other = 1 - core
    barrier = pltpu.get_barrier_semaphore()
    pl.semaphore_signal(barrier, inc=1, device_id=(chip, other, yh, z), device_id_type=MESH_ID)
    pl.semaphore_wait(barrier, 1)
    copy = pltpu.make_async_remote_copy(
        src_ref=x_ref.at[:, pl.ds(other, 1)],
        dst_ref=out_ref,
        send_sem=sems.at[0],
        recv_sem=sems.at[1],
        device_id=(chip, other, yh, z),
        device_id_type=MESH_ID,
    )
    copy.start()
    copy.wait()


def partner_rows(x):
    chips, cores, rows, width = x.shape
    return pl.pallas_call(
        partner_kernel,
        out_shape=jax.ShapeDtypeStruct((chips, 1, rows, width), x.dtype),
        in_specs=[pl.BlockSpec(memory_space=pl.ANY)],
        out_specs=pl.BlockSpec(memory_space=pl.ANY),
        scratch_shapes=[pltpu.SemaphoreType.DMA((2,))],
        compiler_params=pltpu.CompilerParams(collective_id=1, has_side_effects=True),
        cost_estimate=pl.CostEstimate(
            flops=0, transcendentals=0, bytes_accessed=chips * rows * width * x.dtype.itemsize
        ),
    )(x)


def local_slots(routes, expert_count):
    tok = routes.shape[0]
    expert_ids = jnp.arange(expert_count, dtype=jnp.int32)
    hits = routes[:, :, None] == expert_ids
    naming = jnp.sum(hits.astype(jnp.float32), axis=1)
    earlier = (
        jnp.arange(tok, dtype=jnp.int32)[None, :] < jnp.arange(tok, dtype=jnp.int32)[:, None]
    ).astype(jnp.bfloat16)
    before = jnp.dot(earlier, naming.astype(jnp.bfloat16), preferred_element_type=jnp.float32)
    return jnp.sum(jnp.where(hits, before[:, None, :], 0.0), axis=2)


def selection(route_f, slot_f, weight_f, expert, most):
    names = route_f == expert.astype(jnp.float32)
    position = jnp.sum(jnp.where(names, slot_f + 1.0, 0.0), axis=2) - 1.0
    weight = jnp.sum(jnp.where(names, weight_f, 0.0), axis=2)
    picks = position[:, None, :] == jnp.arange(most, dtype=jnp.float32)[None, :, None]
    packed_weight = jnp.sum(jnp.where(picks, weight[:, None, :], 0.0), axis=2)
    return picks.astype(jnp.bfloat16), packed_weight


def block_picks(picks):
    sources, most, tok = picks.shape
    eye = jnp.eye(sources, dtype=picks.dtype)
    return (picks[:, :, None, :] * eye[:, None, :, None]).reshape(sources * most, sources * tok)


def on_device(grad_out, routes, affinity, saved_hidden, down_proj):
    n_yh = lax.axis_size("yh")
    n_z = lax.axis_size("z")
    exp_devices = n_yh * n_z
    local_experts = down_proj.shape[1]
    expert_count = exp_devices * local_experts
    most = saved_hidden.shape[3]
    width = grad_out.shape[1]
    hidden_units = saved_hidden.shape[4]
    topk = routes.shape[1]
    tok = routes.shape[0]
    yh = lax.axis_index("yh")
    z = lax.axis_index("z")
    partner_yh = (yh + 1) % n_yh
    mine = yh * n_z + z
    partner = partner_yh * n_z + z

    totals = jnp.sum(affinity, axis=-1, keepdims=True)
    shares = affinity / totals
    route_weight = (ROUTE_SCALE * shares).astype(jnp.bfloat16)
    slots = local_slots(routes, expert_count)
    meta = jnp.concatenate(
        [
            routes.astype(jnp.bfloat16),
            slots.astype(jnp.bfloat16),
            route_weight,
            jnp.zeros((routes.shape[0], META - 3 * topk), jnp.bfloat16),
        ],
        axis=1,
    )
    half = width // 2
    swap = [(i, (i + 1) % n_yh) for i in range(n_yh)]
    first_part = jnp.concatenate([grad_out[:, :half], meta], axis=1)
    gathered_a = lax.all_gather(first_part, "z", axis=0, tiled=True)
    gathered_w = gather_weight(down_proj.reshape(-1, width)).reshape(hidden_units, width)
    gathered_a, gathered_w = lax.optimization_barrier((gathered_a, gathered_w))
    meta_all = gathered_a[:, half : half + 3 * topk].astype(jnp.float32).reshape(n_z, tok, 3 * topk)
    route_f = meta_all[:, :, 0:topk]
    slot_f = meta_all[:, :, topk : 2 * topk]
    weight_f = meta_all[:, :, 2 * topk : 3 * topk]

    pick_mine, weight_mine = selection(route_f, slot_f, weight_f, mine, most)
    pick_partner, weight_partner = selection(route_f, slot_f, weight_f, partner, most)
    pick_mine = block_picks(pick_mine)
    pick_partner = block_picks(pick_partner)
    weight_far = lax.ppermute(weight_partner, "yh", perm=swap)

    def pack(gathered):
        out = jnp.dot(pick_partner, gathered, preferred_element_type=jnp.float32)
        far = lax.ppermute(out.astype(jnp.bfloat16), "yh", perm=swap)
        near = jnp.dot(pick_mine, gathered, preferred_element_type=jnp.float32)
        return near.astype(jnp.bfloat16), far

    near_a, far_a = pack(gathered_a[:, :half])
    second_part, _ = lax.optimization_barrier((grad_out[:, half:], gathered_a))
    gathered_b = lax.all_gather(second_part, "z", axis=0, tiled=True)
    near_b, far_b = pack(gathered_b)
    near_rows = jnp.concatenate([near_a, near_b], axis=1)
    far_rows = jnp.concatenate([far_a, far_b], axis=1)

    hidden = saved_hidden.reshape(exp_devices, most, hidden_units)
    plane = lambda x, p: lax.dynamic_slice_in_dim(x, p * n_z, n_z, axis=0)
    near_hidden = plane(hidden, yh).reshape(n_z * most, hidden_units)
    far_hidden = plane(hidden, partner_yh).reshape(n_z * most, hidden_units)

    def expert_side(rows, row_weight, hid):
        rows = rows.reshape(n_z * most, width)
        scale = row_weight.reshape(n_z * most, 1)
        projected = jnp.einsum(
            "rd,hd->rh", rows, gathered_w, preferred_element_type=jnp.float32
        )
        hidden_grad = (scale * projected).astype(jnp.bfloat16)
        combine = ROUTE_SCALE * jnp.sum(hid.astype(jnp.float32) * projected, axis=-1)
        scaled = (scale * rows.astype(jnp.float32)).astype(jnp.bfloat16)
        term = jnp.einsum("rh,rd->hd", hid, scaled, preferred_element_type=jnp.float32)
        return hidden_grad, combine, term

    near_grad, near_combine, near_term = expert_side(near_rows, weight_mine, near_hidden)
    far_grad, far_combine, far_term = expert_side(far_rows, weight_far, far_hidden)
    grad_term = near_term + far_term
    n_rc = lax.axis_size("rc")
    n_core = lax.axis_size("core")
    by_chip = grad_term.astype(jnp.bfloat16).reshape(n_rc, n_core, -1, width)
    received = partner_rows(by_chip)
    own = lax.dynamic_slice_in_dim(by_chip, lax.axis_index("core"), 1, axis=1)
    on_chip = (own.astype(jnp.float32) + received.astype(jnp.float32)).astype(jnp.bfloat16)
    down_grad = lax.psum_scatter(
        on_chip.reshape(n_rc, -1, width), "rc", scatter_dimension=0, tiled=True
    ).astype(jnp.float32)

    first = yh == 0
    hidden_grad = jnp.where(
        first,
        jnp.concatenate([near_grad, far_grad], axis=0),
        jnp.concatenate([far_grad, near_grad], axis=0),
    )
    combine_grad = jnp.where(
        first,
        jnp.concatenate([near_combine, far_combine], axis=0),
        jnp.concatenate([far_combine, near_combine], axis=0),
    ).reshape(exp_devices, most)
    returned = lax.all_to_all(
        combine_grad, ("yh", "z"), split_axis=0, concat_axis=0, tiled=True
    )
    expert_ids = jnp.arange(expert_count, dtype=jnp.int32)
    slot_ids = jnp.arange(most, dtype=jnp.float32)
    by_expert = jnp.sum(
        jnp.where((routes[:, :, None] == expert_ids)[:, :, :, None], returned[None, None], 0.0),
        axis=2,
    )
    route_grad = jnp.sum(
        jnp.where(slots[:, :, None] == slot_ids, by_expert, 0.0), axis=2
    )
    affinity_grad = (route_grad - jnp.sum(route_grad * shares, axis=-1, keepdims=True)) / totals
    return (
        affinity_grad,
        hidden_grad.reshape(saved_hidden.shape),
        down_grad.reshape(down_proj.shape),
    )


def solution(mesh):
    n_exp = mesh.shape["exp"]
    n_yh = 2
    n_rep = mesh.shape["rep"]
    split = Mesh(
        mesh.devices.reshape(n_rep // 2, 2, n_yh, n_exp // n_yh),
        ("rc", "core", "yh", "z"),
    )
    return jax.shard_map(
        on_device,
        mesh=split,
        in_specs=(
            P(TOKENS_SPEC, None),
            P(TOKENS_SPEC, None),
            P(TOKENS_SPEC, None),
            P(REP, ("yh", "z"), None, None, None),
            P(REP, ("yh", "z"), None),
        ),
        out_specs=(
            P(TOKENS_SPEC, None),
            P(REP, ("yh", "z"), None, None, None),
            P(REP, ("yh", "z"), None),
        ),
        check_vma=False,
    )
```

```python
import jax
import jax.numpy as jnp
from jax import lax
from jax.experimental import pallas as pl
from jax.experimental.pallas import tpu as pltpu
from jax.sharding import Mesh
from jax.sharding import PartitionSpec as P

ROUTE_SCALE = 2.5
TOKENS_SPEC = ("rc", "core", "yh", "z")
REP = ("rc", "core")
META = 128
MESH_ID = pl.DeviceIdType.MESH


def gather_weight_kernel(n, w_ref, out_ref, send_sem, recv_sem, fwd_send, fwd_recv, own_sem, local_sem):
    chip = lax.axis_index("rc")
    core = lax.axis_index("core")
    yh = lax.axis_index("yh")
    z = lax.axis_index("z")
    chips = n // 2
    me = chip * 2 + core
    partner = chip * 2 + (1 - core)
    barrier = pltpu.get_barrier_semaphore()
    for off in range(1, chips):
        peer = lax.rem(chip + off, chips) * 2 + core
        pl.semaphore_signal(barrier, inc=1, device_id=(peer // 2, peer % 2, yh, z), device_id_type=MESH_ID)
    pl.semaphore_signal(barrier, inc=1, device_id=(partner // 2, partner % 2, yh, z), device_id_type=MESH_ID)
    pl.semaphore_wait(barrier, chips)
    local = pltpu.make_async_copy(w_ref, out_ref.at[me], local_sem)
    local.start()
    own = pltpu.make_async_remote_copy(
        src_ref=w_ref,
        dst_ref=out_ref.at[me],
        send_sem=own_sem.at[0],
        recv_sem=own_sem.at[1],
        device_id=(partner // 2, partner % 2, yh, z),
        device_id_type=MESH_ID,
    )
    own.start()
    sends = []
    for off in range(1, chips):
        peer = lax.rem(chip + off, chips) * 2 + core
        copy = pltpu.make_async_remote_copy(
            src_ref=w_ref,
            dst_ref=out_ref.at[me],
            send_sem=send_sem.at[off],
            recv_sem=recv_sem.at[off],
            device_id=(peer // 2, peer % 2, yh, z),
            device_id_type=MESH_ID,
        )
        copy.start()
        sends.append(copy)
    forwards = []
    for off in range(1, chips):
        source = lax.rem(chip - off + chips, chips) * 2 + core
        incoming = pltpu.make_async_remote_copy(
            src_ref=w_ref,
            dst_ref=out_ref.at[source],
            send_sem=send_sem.at[off],
            recv_sem=recv_sem.at[off],
            device_id=(source // 2, source % 2, yh, z),
            device_id_type=MESH_ID,
        )
        incoming.wait_recv()
        forward = pltpu.make_async_remote_copy(
            src_ref=out_ref.at[source],
            dst_ref=out_ref.at[source],
            send_sem=fwd_send.at[off],
            recv_sem=fwd_recv.at[off],
            device_id=(partner // 2, partner % 2, yh, z),
            device_id_type=MESH_ID,
        )
        forward.start()
        forwards.append(forward)
    for copy in sends:
        copy.wait_send()
    own.wait_send()
    for forward in forwards:
        forward.wait_send()
    partner_own = pltpu.make_async_remote_copy(
        src_ref=w_ref,
        dst_ref=out_ref.at[partner],
        send_sem=own_sem.at[0],
        recv_sem=own_sem.at[1],
        device_id=(partner // 2, partner % 2, yh, z),
        device_id_type=MESH_ID,
    )
    partner_own.wait_recv()
    for off in range(1, chips):
        source = lax.rem(chip - off + chips, chips) * 2 + (1 - core)
        relayed = pltpu.make_async_remote_copy(
            src_ref=out_ref.at[source],
            dst_ref=out_ref.at[source],
            send_sem=fwd_send.at[off],
            recv_sem=fwd_recv.at[off],
            device_id=(partner // 2, partner % 2, yh, z),
            device_id_type=MESH_ID,
        )
        relayed.wait_recv()
    local.wait()


def gather_weight(w):
    n = lax.axis_size("rc") * lax.axis_size("core")
    rows, width = w.shape
    return pl.pallas_call(
        lambda *refs: gather_weight_kernel(n, *refs),
        out_shape=jax.ShapeDtypeStruct((n, rows, width), w.dtype),
        in_specs=[pl.BlockSpec(memory_space=pl.ANY)],
        out_specs=pl.BlockSpec(memory_space=pl.ANY),
        scratch_shapes=[
            pltpu.SemaphoreType.DMA((n // 2,)),
            pltpu.SemaphoreType.DMA((n // 2,)),
            pltpu.SemaphoreType.DMA((n // 2,)),
            pltpu.SemaphoreType.DMA((n // 2,)),
            pltpu.SemaphoreType.DMA((2,)),
            pltpu.SemaphoreType.DMA(()),
        ],
        compiler_params=pltpu.CompilerParams(collective_id=0, has_side_effects=True),
        cost_estimate=pl.CostEstimate(
            flops=0, transcendentals=0, bytes_accessed=2 * n * rows * width * w.dtype.itemsize
        ),
    )(w)


def partner_kernel(x_ref, out_ref, sems):
    chip = lax.axis_index("rc")
    core = lax.axis_index("core")
    yh = lax.axis_index("yh")
    z = lax.axis_index("z")
    other = 1 - core
    barrier = pltpu.get_barrier_semaphore()
    pl.semaphore_signal(barrier, inc=1, device_id=(chip, other, yh, z), device_id_type=MESH_ID)
    pl.semaphore_wait(barrier, 1)
    copy = pltpu.make_async_remote_copy(
        src_ref=x_ref.at[:, pl.ds(other, 1)],
        dst_ref=out_ref,
        send_sem=sems.at[0],
        recv_sem=sems.at[1],
        device_id=(chip, other, yh, z),
        device_id_type=MESH_ID,
    )
    copy.start()
    copy.wait()


def partner_rows(x):
    chips, cores, rows, width = x.shape
    return pl.pallas_call(
        partner_kernel,
        out_shape=jax.ShapeDtypeStruct((chips, 1, rows, width), x.dtype),
        in_specs=[pl.BlockSpec(memory_space=pl.ANY)],
        out_specs=pl.BlockSpec(memory_space=pl.ANY),
        scratch_shapes=[pltpu.SemaphoreType.DMA((2,))],
        compiler_params=pltpu.CompilerParams(collective_id=1, has_side_effects=True),
        cost_estimate=pl.CostEstimate(
            flops=0, transcendentals=0, bytes_accessed=chips * rows * width * x.dtype.itemsize
        ),
    )(x)


def local_slots(routes, expert_count):
    tok = routes.shape[0]
    expert_ids = jnp.arange(expert_count, dtype=jnp.int32)
    hits = routes[:, :, None] == expert_ids
    naming = jnp.sum(hits.astype(jnp.float32), axis=1)
    earlier = (
        jnp.arange(tok, dtype=jnp.int32)[None, :] < jnp.arange(tok, dtype=jnp.int32)[:, None]
    ).astype(jnp.bfloat16)
    before = jnp.dot(earlier, naming.astype(jnp.bfloat16), preferred_element_type=jnp.float32)
    return jnp.sum(jnp.where(hits, before[:, None, :], 0.0), axis=2)


def selection(route_f, slot_f, weight_f, expert, most):
    names = route_f == expert.astype(jnp.float32)
    position = jnp.sum(jnp.where(names, slot_f + 1.0, 0.0), axis=2) - 1.0
    weight = jnp.sum(jnp.where(names, weight_f, 0.0), axis=2)
    picks = position[:, None, :] == jnp.arange(most, dtype=jnp.float32)[None, :, None]
    packed_weight = jnp.sum(jnp.where(picks, weight[:, None, :], 0.0), axis=2)
    return picks.astype(jnp.bfloat16), packed_weight


def block_picks(picks):
    sources, most, tok = picks.shape
    eye = jnp.eye(sources, dtype=picks.dtype)
    return (picks[:, :, None, :] * eye[:, None, :, None]).reshape(sources * most, sources * tok)


def on_device(grad_out, routes, affinity, saved_hidden, down_proj):
    n_yh = lax.axis_size("yh")
    n_z = lax.axis_size("z")
    exp_devices = n_yh * n_z
    local_experts = down_proj.shape[1]
    expert_count = exp_devices * local_experts
    most = saved_hidden.shape[3]
    width = grad_out.shape[1]
    hidden_units = saved_hidden.shape[4]
    topk = routes.shape[1]
    tok = routes.shape[0]
    yh = lax.axis_index("yh")
    z = lax.axis_index("z")
    partner_yh = (yh + 1) % n_yh
    mine = yh * n_z + z
    partner = partner_yh * n_z + z

    totals = jnp.sum(affinity, axis=-1, keepdims=True)
    shares = affinity / totals
    route_weight = (ROUTE_SCALE * shares).astype(jnp.bfloat16)
    slots = local_slots(routes, expert_count)
    meta = jnp.concatenate(
        [
            routes.astype(jnp.bfloat16),
            slots.astype(jnp.bfloat16),
            route_weight,
            jnp.zeros((routes.shape[0], META - 3 * topk), jnp.bfloat16),
        ],
        axis=1,
    )
    half = width // 2
    swap = [(i, (i + 1) % n_yh) for i in range(n_yh)]
    first_part = jnp.concatenate([grad_out[:, :half], meta], axis=1)
    gathered_a = lax.all_gather(first_part, "z", axis=0, tiled=True)
    gathered_w = gather_weight(down_proj.reshape(-1, width)).reshape(hidden_units, width)
    gathered_a, gathered_w = lax.optimization_barrier((gathered_a, gathered_w))
    meta_all = gathered_a[:, half : half + 3 * topk].astype(jnp.float32).reshape(n_z, tok, 3 * topk)
    route_f = meta_all[:, :, 0:topk]
    slot_f = meta_all[:, :, topk : 2 * topk]
    weight_f = meta_all[:, :, 2 * topk : 3 * topk]

    pick_mine, weight_mine = selection(route_f, slot_f, weight_f, mine, most)
    pick_partner, weight_partner = selection(route_f, slot_f, weight_f, partner, most)
    pick_mine = block_picks(pick_mine)
    pick_partner = block_picks(pick_partner)
    weight_far = lax.ppermute(weight_partner, "yh", perm=swap)

    def pack(gathered):
        out = jnp.dot(pick_partner, gathered, preferred_element_type=jnp.float32)
        out, _ = lax.optimization_barrier((out.astype(jnp.bfloat16), weight_far))
        far = lax.ppermute(out, "yh", perm=swap)
        near = jnp.dot(pick_mine, gathered, preferred_element_type=jnp.float32)
        return near.astype(jnp.bfloat16), far

    near_a, far_a = pack(gathered_a[:, :half])
    second_part, _ = lax.optimization_barrier((grad_out[:, half:], gathered_a))
    gathered_b = lax.all_gather(second_part, "z", axis=0, tiled=True)
    near_b, far_b = pack(gathered_b)
    near_rows = jnp.concatenate([near_a, near_b], axis=1)

    hidden = saved_hidden.reshape(exp_devices, most, hidden_units)
    plane = lambda x, p: lax.dynamic_slice_in_dim(x, p * n_z, n_z, axis=0)
    near_hidden = plane(hidden, yh).reshape(n_z * most, hidden_units)
    far_hidden = plane(hidden, partner_yh).reshape(n_z * most, hidden_units)

    def expert_side(rows, row_weight, hid):
        rows = rows.reshape(n_z * most, width)
        scale = row_weight.reshape(n_z * most, 1)
        projected = jnp.einsum(
            "rd,hd->rh", rows, gathered_w, preferred_element_type=jnp.float32
        )
        hidden_grad = (scale * projected).astype(jnp.bfloat16)
        combine = ROUTE_SCALE * jnp.sum(hid.astype(jnp.float32) * projected, axis=-1)
        scaled = (scale * rows.astype(jnp.float32)).astype(jnp.bfloat16)
        term = jnp.einsum("rh,rd->hd", hid, scaled, preferred_element_type=jnp.float32)
        return hidden_grad, combine, term

    near_grad, near_combine, near_term = expert_side(near_rows, weight_mine, near_hidden)
    far_scale = weight_far.reshape(n_z * most, 1)

    def far_part(rows, w_cols):
        projected = jnp.einsum("rd,hd->rh", rows, w_cols, preferred_element_type=jnp.float32)
        scaled = (far_scale * rows.astype(jnp.float32)).astype(jnp.bfloat16)
        term = jnp.einsum("rh,rd->hd", far_hidden, scaled, preferred_element_type=jnp.float32)
        return projected, term

    far_proj_a, far_term_a = far_part(far_a, gathered_w[:, :half])
    far_proj_b, far_term_b = far_part(far_b, gathered_w[:, half:])
    far_proj = far_proj_a + far_proj_b
    far_grad = (far_scale * far_proj).astype(jnp.bfloat16)
    far_combine = ROUTE_SCALE * jnp.sum(far_hidden.astype(jnp.float32) * far_proj, axis=-1)
    grad_term = near_term + jnp.concatenate([far_term_a, far_term_b], axis=1)
    n_rc = lax.axis_size("rc")
    n_core = lax.axis_size("core")
    by_chip = grad_term.astype(jnp.bfloat16).reshape(n_rc, n_core, -1, width)
    received = partner_rows(by_chip)
    own = lax.dynamic_slice_in_dim(by_chip, lax.axis_index("core"), 1, axis=1)
    on_chip = (own.astype(jnp.float32) + received.astype(jnp.float32)).astype(jnp.bfloat16)
    down_grad = lax.psum_scatter(
        on_chip.reshape(n_rc, -1, width), "rc", scatter_dimension=0, tiled=True
    ).astype(jnp.float32)

    first = yh == 0
    hidden_grad = jnp.where(
        first,
        jnp.concatenate([near_grad, far_grad], axis=0),
        jnp.concatenate([far_grad, near_grad], axis=0),
    )
    combine_grad = jnp.where(
        first,
        jnp.concatenate([near_combine, far_combine], axis=0),
        jnp.concatenate([far_combine, near_combine], axis=0),
    ).reshape(exp_devices, most)
    returned = lax.all_to_all(
        combine_grad, ("yh", "z"), split_axis=0, concat_axis=0, tiled=True
    )
    expert_ids = jnp.arange(expert_count, dtype=jnp.int32)
    slot_ids = jnp.arange(most, dtype=jnp.float32)
    by_expert = jnp.sum(
        jnp.where((routes[:, :, None] == expert_ids)[:, :, :, None], returned[None, None], 0.0),
        axis=2,
    )
    route_grad = jnp.sum(
        jnp.where(slots[:, :, None] == slot_ids, by_expert, 0.0), axis=2
    )
    affinity_grad = (route_grad - jnp.sum(route_grad * shares, axis=-1, keepdims=True)) / totals
    return (
        affinity_grad,
        hidden_grad.reshape(saved_hidden.shape),
        down_grad.reshape(down_proj.shape),
    )


def solution(mesh):
    n_exp = mesh.shape["exp"]
    n_yh = 2
    n_rep = mesh.shape["rep"]
    split = Mesh(
        mesh.devices.reshape(n_rep // 2, 2, n_yh, n_exp // n_yh),
        ("rc", "core", "yh", "z"),
    )
    return jax.shard_map(
        on_device,
        mesh=split,
        in_specs=(
            P(TOKENS_SPEC, None),
            P(TOKENS_SPEC, None),
            P(TOKENS_SPEC, None),
            P(REP, ("yh", "z"), None, None, None),
            P(REP, ("yh", "z"), None),
        ),
        out_specs=(
            P(TOKENS_SPEC, None),
            P(REP, ("yh", "z"), None, None, None),
            P(REP, ("yh", "z"), None),
        ),
        check_vma=False,
    )
```

```python
import jax
import jax.numpy as jnp
from jax import lax
from jax.experimental import pallas as pl
from jax.experimental.pallas import tpu as pltpu
from jax.sharding import Mesh
from jax.sharding import PartitionSpec as P

ROUTE_SCALE = 2.5
TOKENS_SPEC = ("rc", "core", "yh", "z")
REP = ("rc", "core")
META = 128
MESH_ID = pl.DeviceIdType.MESH


def gather_weight_kernel(n, w_ref, out_ref, send_sem, recv_sem, fwd_send, fwd_recv, own_sem, local_sem):
    chip = lax.axis_index("rc")
    core = lax.axis_index("core")
    yh = lax.axis_index("yh")
    z = lax.axis_index("z")
    chips = n // 2
    me = chip * 2 + core
    partner = chip * 2 + (1 - core)
    barrier = pltpu.get_barrier_semaphore()
    for off in range(1, chips):
        peer = lax.rem(chip + off, chips) * 2 + core
        pl.semaphore_signal(barrier, inc=1, device_id=(peer // 2, peer % 2, yh, z), device_id_type=MESH_ID)
    pl.semaphore_signal(barrier, inc=1, device_id=(partner // 2, partner % 2, yh, z), device_id_type=MESH_ID)
    pl.semaphore_wait(barrier, chips)
    local = pltpu.make_async_copy(w_ref, out_ref.at[me], local_sem)
    local.start()
    own = pltpu.make_async_remote_copy(
        src_ref=w_ref,
        dst_ref=out_ref.at[me],
        send_sem=own_sem.at[0],
        recv_sem=own_sem.at[1],
        device_id=(partner // 2, partner % 2, yh, z),
        device_id_type=MESH_ID,
    )
    own.start()
    sends = []
    for off in range(1, chips):
        peer = lax.rem(chip + off, chips) * 2 + core
        copy = pltpu.make_async_remote_copy(
            src_ref=w_ref,
            dst_ref=out_ref.at[me],
            send_sem=send_sem.at[off],
            recv_sem=recv_sem.at[off],
            device_id=(peer // 2, peer % 2, yh, z),
            device_id_type=MESH_ID,
        )
        copy.start()
        sends.append(copy)
    forwards = []
    for off in range(1, chips):
        source = lax.rem(chip - off + chips, chips) * 2 + core
        incoming = pltpu.make_async_remote_copy(
            src_ref=w_ref,
            dst_ref=out_ref.at[source],
            send_sem=send_sem.at[off],
            recv_sem=recv_sem.at[off],
            device_id=(source // 2, source % 2, yh, z),
            device_id_type=MESH_ID,
        )
        incoming.wait_recv()
        forward = pltpu.make_async_remote_copy(
            src_ref=out_ref.at[source],
            dst_ref=out_ref.at[source],
            send_sem=fwd_send.at[off],
            recv_sem=fwd_recv.at[off],
            device_id=(partner // 2, partner % 2, yh, z),
            device_id_type=MESH_ID,
        )
        forward.start()
        forwards.append(forward)
    for copy in sends:
        copy.wait_send()
    own.wait_send()
    for forward in forwards:
        forward.wait_send()
    partner_own = pltpu.make_async_remote_copy(
        src_ref=w_ref,
        dst_ref=out_ref.at[partner],
        send_sem=own_sem.at[0],
        recv_sem=own_sem.at[1],
        device_id=(partner // 2, partner % 2, yh, z),
        device_id_type=MESH_ID,
    )
    partner_own.wait_recv()
    for off in range(1, chips):
        source = lax.rem(chip - off + chips, chips) * 2 + (1 - core)
        relayed = pltpu.make_async_remote_copy(
            src_ref=out_ref.at[source],
            dst_ref=out_ref.at[source],
            send_sem=fwd_send.at[off],
            recv_sem=fwd_recv.at[off],
            device_id=(partner // 2, partner % 2, yh, z),
            device_id_type=MESH_ID,
        )
        relayed.wait_recv()
    local.wait()


def gather_weight(w):
    n = lax.axis_size("rc") * lax.axis_size("core")
    rows, width = w.shape
    return pl.pallas_call(
        lambda *refs: gather_weight_kernel(n, *refs),
        out_shape=jax.ShapeDtypeStruct((n, rows, width), w.dtype),
        in_specs=[pl.BlockSpec(memory_space=pl.ANY)],
        out_specs=pl.BlockSpec(memory_space=pl.ANY),
        scratch_shapes=[
            pltpu.SemaphoreType.DMA((n // 2,)),
            pltpu.SemaphoreType.DMA((n // 2,)),
            pltpu.SemaphoreType.DMA((n // 2,)),
            pltpu.SemaphoreType.DMA((n // 2,)),
            pltpu.SemaphoreType.DMA((2,)),
            pltpu.SemaphoreType.DMA(()),
        ],
        compiler_params=pltpu.CompilerParams(collective_id=0, has_side_effects=True),
        cost_estimate=pl.CostEstimate(
            flops=0, transcendentals=0, bytes_accessed=2 * n * rows * width * w.dtype.itemsize
        ),
    )(w)


def partner_kernel(x_ref, out_ref, sems):
    chip = lax.axis_index("rc")
    core = lax.axis_index("core")
    yh = lax.axis_index("yh")
    z = lax.axis_index("z")
    other = 1 - core
    barrier = pltpu.get_barrier_semaphore()
    pl.semaphore_signal(barrier, inc=1, device_id=(chip, other, yh, z), device_id_type=MESH_ID)
    pl.semaphore_wait(barrier, 1)
    copy = pltpu.make_async_remote_copy(
        src_ref=x_ref.at[:, pl.ds(other, 1)],
        dst_ref=out_ref,
        send_sem=sems.at[0],
        recv_sem=sems.at[1],
        device_id=(chip, other, yh, z),
        device_id_type=MESH_ID,
    )
    copy.start()
    copy.wait()


def partner_rows(x):
    chips, cores, rows, width = x.shape
    return pl.pallas_call(
        partner_kernel,
        out_shape=jax.ShapeDtypeStruct((chips, 1, rows, width), x.dtype),
        in_specs=[pl.BlockSpec(memory_space=pl.ANY)],
        out_specs=pl.BlockSpec(memory_space=pl.ANY),
        scratch_shapes=[pltpu.SemaphoreType.DMA((2,))],
        compiler_params=pltpu.CompilerParams(collective_id=1, has_side_effects=True),
        cost_estimate=pl.CostEstimate(
            flops=0, transcendentals=0, bytes_accessed=chips * rows * width * x.dtype.itemsize
        ),
    )(x)


def local_slots(routes, expert_count):
    tok = routes.shape[0]
    expert_ids = jnp.arange(expert_count, dtype=jnp.int32)
    hits = routes[:, :, None] == expert_ids
    naming = jnp.sum(hits.astype(jnp.float32), axis=1)
    earlier = (
        jnp.arange(tok, dtype=jnp.int32)[None, :] < jnp.arange(tok, dtype=jnp.int32)[:, None]
    ).astype(jnp.bfloat16)
    before = jnp.dot(earlier, naming.astype(jnp.bfloat16), preferred_element_type=jnp.float32)
    return jnp.sum(jnp.where(hits, before[:, None, :], 0.0), axis=2)


def selection(route_f, slot_f, weight_f, expert, most):
    names = route_f == expert.astype(jnp.float32)
    position = jnp.sum(jnp.where(names, slot_f + 1.0, 0.0), axis=2) - 1.0
    weight = jnp.sum(jnp.where(names, weight_f, 0.0), axis=2)
    picks = position[:, None, :] == jnp.arange(most, dtype=jnp.float32)[None, :, None]
    packed_weight = jnp.sum(jnp.where(picks, weight[:, None, :], 0.0), axis=2)
    return picks.astype(jnp.bfloat16), packed_weight


def block_picks(picks):
    sources, most, tok = picks.shape
    eye = jnp.eye(sources, dtype=picks.dtype)
    return (picks[:, :, None, :] * eye[:, None, :, None]).reshape(sources * most, sources * tok)


def on_device(grad_out, routes, affinity, saved_hidden, down_proj):
    n_yh = lax.axis_size("yh")
    n_z = lax.axis_size("z")
    exp_devices = n_yh * n_z
    local_experts = down_proj.shape[1]
    expert_count = exp_devices * local_experts
    most = saved_hidden.shape[3]
    width = grad_out.shape[1]
    hidden_units = saved_hidden.shape[4]
    topk = routes.shape[1]
    tok = routes.shape[0]
    yh = lax.axis_index("yh")
    z = lax.axis_index("z")
    partner_yh = (yh + 1) % n_yh
    mine = yh * n_z + z
    partner = partner_yh * n_z + z

    totals = jnp.sum(affinity, axis=-1, keepdims=True)
    shares = affinity / totals
    route_weight = (ROUTE_SCALE * shares).astype(jnp.bfloat16)
    slots = local_slots(routes, expert_count)
    meta = jnp.concatenate(
        [
            routes.astype(jnp.bfloat16),
            slots.astype(jnp.bfloat16),
            route_weight,
            jnp.zeros((routes.shape[0], META - 3 * topk), jnp.bfloat16),
        ],
        axis=1,
    )
    half = width // 2
    swap = [(i, (i + 1) % n_yh) for i in range(n_yh)]
    first_part = jnp.concatenate([grad_out[:, :half], meta], axis=1)
    gathered_a = lax.all_gather(first_part, "z", axis=0, tiled=True)
    gathered_w = gather_weight(down_proj.reshape(-1, width)).reshape(hidden_units, width)
    gathered_a, gathered_w = lax.optimization_barrier((gathered_a, gathered_w))
    meta_all = gathered_a[:, half : half + 3 * topk].astype(jnp.float32).reshape(n_z, tok, 3 * topk)
    route_f = meta_all[:, :, 0:topk]
    slot_f = meta_all[:, :, topk : 2 * topk]
    weight_f = meta_all[:, :, 2 * topk : 3 * topk]

    pick_mine, weight_mine = selection(route_f, slot_f, weight_f, mine, most)
    pick_partner, weight_partner = selection(route_f, slot_f, weight_f, partner, most)
    pick_mine = block_picks(pick_mine)
    pick_partner = block_picks(pick_partner)
    weight_far = lax.ppermute(weight_partner, "yh", perm=swap)

    def pack(gathered):
        out = jnp.dot(pick_partner, gathered, preferred_element_type=jnp.float32)
        far = lax.ppermute(out.astype(jnp.bfloat16), "yh", perm=swap)
        near = jnp.dot(pick_mine, gathered, preferred_element_type=jnp.float32)
        return near.astype(jnp.bfloat16), far

    near_a, far_a = pack(gathered_a[:, :half])
    gathered_b = lax.all_gather(grad_out[:, half:], "z", axis=0, tiled=True)
    near_b, far_b = pack(gathered_b)
    near_rows = jnp.concatenate([near_a, near_b], axis=1)
    far_rows = jnp.concatenate([far_a, far_b], axis=1)

    hidden = saved_hidden.reshape(exp_devices, most, hidden_units)
    plane = lambda x, p: lax.dynamic_slice_in_dim(x, p * n_z, n_z, axis=0)
    near_hidden = plane(hidden, yh).reshape(n_z * most, hidden_units)
    far_hidden = plane(hidden, partner_yh).reshape(n_z * most, hidden_units)

    def expert_side(rows, row_weight, hid):
        rows = rows.reshape(n_z * most, width)
        scale = row_weight.reshape(n_z * most, 1)
        projected = jnp.einsum(
            "rd,hd->rh", rows, gathered_w, preferred_element_type=jnp.float32
        )
        hidden_grad = (scale * projected).astype(jnp.bfloat16)
        combine = ROUTE_SCALE * jnp.sum(hid.astype(jnp.float32) * projected, axis=-1)
        scaled = (scale * rows.astype(jnp.float32)).astype(jnp.bfloat16)
        term = jnp.einsum("rh,rd->hd", hid, scaled, preferred_element_type=jnp.float32)
        return hidden_grad, combine, term

    near_grad, near_combine, near_term = expert_side(near_rows, weight_mine, near_hidden)
    far_grad, far_combine, far_term = expert_side(far_rows, weight_far, far_hidden)
    grad_term = near_term + far_term
    n_rc = lax.axis_size("rc")
    n_core = lax.axis_size("core")
    by_chip = grad_term.astype(jnp.bfloat16).reshape(n_rc, n_core, -1, width)
    received = partner_rows(by_chip)
    own = lax.dynamic_slice_in_dim(by_chip, lax.axis_index("core"), 1, axis=1)
    on_chip = (own.astype(jnp.float32) + received.astype(jnp.float32)).astype(jnp.bfloat16)
    down_grad = lax.psum_scatter(
        on_chip.reshape(n_rc, -1, width), "rc", scatter_dimension=0, tiled=True
    ).astype(jnp.float32)

    first = yh == 0
    hidden_grad = jnp.where(
        first,
        jnp.concatenate([near_grad, far_grad], axis=0),
        jnp.concatenate([far_grad, near_grad], axis=0),
    )
    combine_grad = jnp.where(
        first,
        jnp.concatenate([near_combine, far_combine], axis=0),
        jnp.concatenate([far_combine, near_combine], axis=0),
    ).reshape(exp_devices, most)
    returned = lax.all_to_all(
        combine_grad, ("yh", "z"), split_axis=0, concat_axis=0, tiled=True
    )
    expert_ids = jnp.arange(expert_count, dtype=jnp.int32)
    slot_ids = jnp.arange(most, dtype=jnp.float32)
    by_expert = jnp.sum(
        jnp.where((routes[:, :, None] == expert_ids)[:, :, :, None], returned[None, None], 0.0),
        axis=2,
    )
    route_grad = jnp.sum(
        jnp.where(slots[:, :, None] == slot_ids, by_expert, 0.0), axis=2
    )
    affinity_grad = (route_grad - jnp.sum(route_grad * shares, axis=-1, keepdims=True)) / totals
    return (
        affinity_grad,
        hidden_grad.reshape(saved_hidden.shape),
        down_grad.reshape(down_proj.shape),
    )


def solution(mesh):
    n_exp = mesh.shape["exp"]
    n_yh = 2
    n_rep = mesh.shape["rep"]
    split = Mesh(
        mesh.devices.reshape(n_rep // 2, 2, n_yh, n_exp // n_yh),
        ("rc", "core", "yh", "z"),
    )
    return jax.shard_map(
        on_device,
        mesh=split,
        in_specs=(
            P(TOKENS_SPEC, None),
            P(TOKENS_SPEC, None),
            P(TOKENS_SPEC, None),
            P(REP, ("yh", "z"), None, None, None),
            P(REP, ("yh", "z"), None),
        ),
        out_specs=(
            P(TOKENS_SPEC, None),
            P(REP, ("yh", "z"), None, None, None),
            P(REP, ("yh", "z"), None),
        ),
        check_vma=False,
    )
```

```python
import jax
import jax.numpy as jnp
from jax import lax
from jax.experimental import pallas as pl
from jax.experimental.pallas import tpu as pltpu
from jax.sharding import Mesh
from jax.sharding import PartitionSpec as P

ROUTE_SCALE = 2.5
TOKENS_SPEC = ("rc", "core", "yh", "z")
REP = ("rc", "core")
META = 128
MESH_ID = pl.DeviceIdType.MESH


def gather_weight_kernel(n, w_ref, out_ref, send_sem, recv_sem, fwd_send, fwd_recv, own_sem, local_sem):
    chip = lax.axis_index("rc")
    core = lax.axis_index("core")
    yh = lax.axis_index("yh")
    z = lax.axis_index("z")
    chips = n // 2
    me = chip * 2 + core
    partner = chip * 2 + (1 - core)
    barrier = pltpu.get_barrier_semaphore()
    for off in range(1, chips):
        peer = lax.rem(chip + off, chips) * 2 + core
        pl.semaphore_signal(barrier, inc=1, device_id=(peer // 2, peer % 2, yh, z), device_id_type=MESH_ID)
    pl.semaphore_signal(barrier, inc=1, device_id=(partner // 2, partner % 2, yh, z), device_id_type=MESH_ID)
    pl.semaphore_wait(barrier, chips)
    local = pltpu.make_async_copy(w_ref, out_ref.at[me], local_sem)
    local.start()
    own = pltpu.make_async_remote_copy(
        src_ref=w_ref,
        dst_ref=out_ref.at[me],
        send_sem=own_sem.at[0],
        recv_sem=own_sem.at[1],
        device_id=(partner // 2, partner % 2, yh, z),
        device_id_type=MESH_ID,
    )
    own.start()
    sends = []
    for off in range(1, chips):
        peer = lax.rem(chip + off, chips) * 2 + core
        copy = pltpu.make_async_remote_copy(
            src_ref=w_ref,
            dst_ref=out_ref.at[me],
            send_sem=send_sem.at[off],
            recv_sem=recv_sem.at[off],
            device_id=(peer // 2, peer % 2, yh, z),
            device_id_type=MESH_ID,
        )
        copy.start()
        sends.append(copy)
    forwards = []
    for off in range(1, chips):
        source = lax.rem(chip - off + chips, chips) * 2 + core
        incoming = pltpu.make_async_remote_copy(
            src_ref=w_ref,
            dst_ref=out_ref.at[source],
            send_sem=send_sem.at[off],
            recv_sem=recv_sem.at[off],
            device_id=(source // 2, source % 2, yh, z),
            device_id_type=MESH_ID,
        )
        incoming.wait_recv()
        forward = pltpu.make_async_remote_copy(
            src_ref=out_ref.at[source],
            dst_ref=out_ref.at[source],
            send_sem=fwd_send.at[off],
            recv_sem=fwd_recv.at[off],
            device_id=(partner // 2, partner % 2, yh, z),
            device_id_type=MESH_ID,
        )
        forward.start()
        forwards.append(forward)
    for copy in sends:
        copy.wait_send()
    own.wait_send()
    for forward in forwards:
        forward.wait_send()
    partner_own = pltpu.make_async_remote_copy(
        src_ref=w_ref,
        dst_ref=out_ref.at[partner],
        send_sem=own_sem.at[0],
        recv_sem=own_sem.at[1],
        device_id=(partner // 2, partner % 2, yh, z),
        device_id_type=MESH_ID,
    )
    partner_own.wait_recv()
    for off in range(1, chips):
        source = lax.rem(chip - off + chips, chips) * 2 + (1 - core)
        relayed = pltpu.make_async_remote_copy(
            src_ref=out_ref.at[source],
            dst_ref=out_ref.at[source],
            send_sem=fwd_send.at[off],
            recv_sem=fwd_recv.at[off],
            device_id=(partner // 2, partner % 2, yh, z),
            device_id_type=MESH_ID,
        )
        relayed.wait_recv()
    local.wait()


def gather_weight(w):
    n = lax.axis_size("rc") * lax.axis_size("core")
    rows, width = w.shape
    return pl.pallas_call(
        lambda *refs: gather_weight_kernel(n, *refs),
        out_shape=jax.ShapeDtypeStruct((n, rows, width), w.dtype),
        in_specs=[pl.BlockSpec(memory_space=pl.ANY)],
        out_specs=pl.BlockSpec(memory_space=pl.ANY),
        scratch_shapes=[
            pltpu.SemaphoreType.DMA((n // 2,)),
            pltpu.SemaphoreType.DMA((n // 2,)),
            pltpu.SemaphoreType.DMA((n // 2,)),
            pltpu.SemaphoreType.DMA((n // 2,)),
            pltpu.SemaphoreType.DMA((2,)),
            pltpu.SemaphoreType.DMA(()),
        ],
        compiler_params=pltpu.CompilerParams(collective_id=0, has_side_effects=True),
        cost_estimate=pl.CostEstimate(
            flops=0, transcendentals=0, bytes_accessed=2 * n * rows * width * w.dtype.itemsize
        ),
    )(w)


def partner_kernel(x_ref, out_ref, sems):
    chip = lax.axis_index("rc")
    core = lax.axis_index("core")
    yh = lax.axis_index("yh")
    z = lax.axis_index("z")
    other = 1 - core
    barrier = pltpu.get_barrier_semaphore()
    pl.semaphore_signal(barrier, inc=1, device_id=(chip, other, yh, z), device_id_type=MESH_ID)
    pl.semaphore_wait(barrier, 1)
    copy = pltpu.make_async_remote_copy(
        src_ref=x_ref.at[:, pl.ds(other, 1)],
        dst_ref=out_ref,
        send_sem=sems.at[0],
        recv_sem=sems.at[1],
        device_id=(chip, other, yh, z),
        device_id_type=MESH_ID,
    )
    copy.start()
    copy.wait()


def partner_rows(x):
    chips, cores, rows, width = x.shape
    return pl.pallas_call(
        partner_kernel,
        out_shape=jax.ShapeDtypeStruct((chips, 1, rows, width), x.dtype),
        in_specs=[pl.BlockSpec(memory_space=pl.ANY)],
        out_specs=pl.BlockSpec(memory_space=pl.ANY),
        scratch_shapes=[pltpu.SemaphoreType.DMA((2,))],
        compiler_params=pltpu.CompilerParams(collective_id=1, has_side_effects=True),
        cost_estimate=pl.CostEstimate(
            flops=0, transcendentals=0, bytes_accessed=chips * rows * width * x.dtype.itemsize
        ),
    )(x)


def local_slots(routes, expert_count):
    tok = routes.shape[0]
    expert_ids = jnp.arange(expert_count, dtype=jnp.int32)
    hits = routes[:, :, None] == expert_ids
    naming = jnp.sum(hits.astype(jnp.float32), axis=1)
    earlier = (
        jnp.arange(tok, dtype=jnp.int32)[None, :] < jnp.arange(tok, dtype=jnp.int32)[:, None]
    ).astype(jnp.bfloat16)
    before = jnp.dot(earlier, naming.astype(jnp.bfloat16), preferred_element_type=jnp.float32)
    return jnp.sum(jnp.where(hits, before[:, None, :], 0.0), axis=2)


def selection(route_f, slot_f, weight_f, expert, most):
    names = route_f == expert.astype(jnp.float32)
    position = jnp.sum(jnp.where(names, slot_f + 1.0, 0.0), axis=2) - 1.0
    weight = jnp.sum(jnp.where(names, weight_f, 0.0), axis=2)
    picks = position[:, None, :] == jnp.arange(most, dtype=jnp.float32)[None, :, None]
    packed_weight = jnp.sum(jnp.where(picks, weight[:, None, :], 0.0), axis=2)
    return picks.astype(jnp.bfloat16), packed_weight


def block_picks(picks):
    sources, most, tok = picks.shape
    eye = jnp.eye(sources, dtype=picks.dtype)
    return (picks[:, :, None, :] * eye[:, None, :, None]).reshape(sources * most, sources * tok)


def on_device(grad_out, routes, affinity, saved_hidden, down_proj):
    n_yh = lax.axis_size("yh")
    n_z = lax.axis_size("z")
    exp_devices = n_yh * n_z
    local_experts = down_proj.shape[1]
    expert_count = exp_devices * local_experts
    most = saved_hidden.shape[3]
    width = grad_out.shape[1]
    hidden_units = saved_hidden.shape[4]
    topk = routes.shape[1]
    tok = routes.shape[0]
    yh = lax.axis_index("yh")
    z = lax.axis_index("z")
    partner_yh = (yh + 1) % n_yh
    mine = yh * n_z + z
    partner = partner_yh * n_z + z

    totals = jnp.sum(affinity, axis=-1, keepdims=True)
    shares = affinity / totals
    route_weight = (ROUTE_SCALE * shares).astype(jnp.bfloat16)
    slots = local_slots(routes, expert_count)
    meta = jnp.concatenate(
        [
            routes.astype(jnp.bfloat16),
            slots.astype(jnp.bfloat16),
            route_weight,
            jnp.zeros((routes.shape[0], META - 3 * topk), jnp.bfloat16),
        ],
        axis=1,
    )
    half = width // 2
    swap = [(i, (i + 1) % n_yh) for i in range(n_yh)]
    first_part = jnp.concatenate([grad_out[:, :half], meta], axis=1)
    gathered_a = lax.all_gather(first_part, "z", axis=0, tiled=True)
    gathered_w = gather_weight(down_proj.reshape(-1, width)).reshape(hidden_units, width)
    gathered_a, gathered_w = lax.optimization_barrier((gathered_a, gathered_w))
    meta_all = gathered_a[:, half : half + 3 * topk].astype(jnp.float32).reshape(n_z, tok, 3 * topk)
    route_f = meta_all[:, :, 0:topk]
    slot_f = meta_all[:, :, topk : 2 * topk]
    weight_f = meta_all[:, :, 2 * topk : 3 * topk]

    pick_mine, weight_mine = selection(route_f, slot_f, weight_f, mine, most)
    pick_partner, weight_partner = selection(route_f, slot_f, weight_f, partner, most)
    pick_mine = block_picks(pick_mine)
    pick_partner = block_picks(pick_partner)

    def pack(gathered, extra=None):
        out = jnp.dot(pick_partner, gathered, preferred_element_type=jnp.float32)
        out = out.astype(jnp.bfloat16)
        if extra is not None:
            out = jnp.concatenate([out, extra], axis=1)
        far = lax.ppermute(out, "yh", perm=swap)
        near = jnp.dot(pick_mine, gathered, preferred_element_type=jnp.float32)
        return near.astype(jnp.bfloat16), far

    weight_cols = jnp.zeros((n_z * most, META), jnp.bfloat16).at[:, 0].set(
        weight_partner.reshape(-1).astype(jnp.bfloat16)
    )
    near_a, far_ext = pack(gathered_a[:, :half], weight_cols)
    far_a = far_ext[:, :half]
    weight_far = far_ext[:, half].astype(jnp.float32)
    gathered_b = lax.all_gather(grad_out[:, half:], "z", axis=0, tiled=True)
    near_b, far_b = pack(gathered_b)
    near_rows = jnp.concatenate([near_a, near_b], axis=1)

    hidden = saved_hidden.reshape(exp_devices, most, hidden_units)
    plane = lambda x, p: lax.dynamic_slice_in_dim(x, p * n_z, n_z, axis=0)
    near_hidden = plane(hidden, yh).reshape(n_z * most, hidden_units)
    far_hidden = plane(hidden, partner_yh).reshape(n_z * most, hidden_units)

    def expert_side(rows, row_weight, hid):
        rows = rows.reshape(n_z * most, width)
        scale = row_weight.reshape(n_z * most, 1)
        projected = jnp.einsum(
            "rd,hd->rh", rows, gathered_w, preferred_element_type=jnp.float32
        )
        hidden_grad = (scale * projected).astype(jnp.bfloat16)
        combine = ROUTE_SCALE * jnp.sum(hid.astype(jnp.float32) * projected, axis=-1)
        scaled = (scale * rows.astype(jnp.float32)).astype(jnp.bfloat16)
        term = jnp.einsum("rh,rd->hd", hid, scaled, preferred_element_type=jnp.float32)
        return hidden_grad, combine, term

    near_grad, near_combine, near_term = expert_side(near_rows, weight_mine, near_hidden)
    far_scale = weight_far.reshape(n_z * most, 1)

    def far_part(rows, w_cols):
        projected = jnp.einsum("rd,hd->rh", rows, w_cols, preferred_element_type=jnp.float32)
        scaled = (far_scale * rows.astype(jnp.float32)).astype(jnp.bfloat16)
        term = jnp.einsum("rh,rd->hd", far_hidden, scaled, preferred_element_type=jnp.float32)
        return projected, term

    far_proj_a, far_term_a = far_part(far_a, gathered_w[:, :half])
    far_proj_b, far_term_b = far_part(far_b, gathered_w[:, half:])
    far_proj = far_proj_a + far_proj_b
    far_grad = (far_scale * far_proj).astype(jnp.bfloat16)
    far_combine = ROUTE_SCALE * jnp.sum(far_hidden.astype(jnp.float32) * far_proj, axis=-1)
    grad_term = near_term + jnp.concatenate([far_term_a, far_term_b], axis=1)
    n_rc = lax.axis_size("rc")
    n_core = lax.axis_size("core")
    by_chip = grad_term.astype(jnp.bfloat16).reshape(n_rc, n_core, -1, width)
    received = partner_rows(by_chip)
    own = lax.dynamic_slice_in_dim(by_chip, lax.axis_index("core"), 1, axis=1)
    on_chip = (own.astype(jnp.float32) + received.astype(jnp.float32)).astype(jnp.bfloat16)
    down_grad = lax.psum_scatter(
        on_chip.reshape(n_rc, -1, width), "rc", scatter_dimension=0, tiled=True
    ).astype(jnp.float32)

    first = yh == 0
    hidden_grad = jnp.where(
        first,
        jnp.concatenate([near_grad, far_grad], axis=0),
        jnp.concatenate([far_grad, near_grad], axis=0),
    )
    combine_grad = jnp.where(
        first,
        jnp.concatenate([near_combine, far_combine], axis=0),
        jnp.concatenate([far_combine, near_combine], axis=0),
    ).reshape(exp_devices, most)
    returned = lax.all_to_all(
        combine_grad, ("yh", "z"), split_axis=0, concat_axis=0, tiled=True
    )
    expert_ids = jnp.arange(expert_count, dtype=jnp.int32)
    slot_ids = jnp.arange(most, dtype=jnp.float32)
    by_expert = jnp.sum(
        jnp.where((routes[:, :, None] == expert_ids)[:, :, :, None], returned[None, None], 0.0),
        axis=2,
    )
    route_grad = jnp.sum(
        jnp.where(slots[:, :, None] == slot_ids, by_expert, 0.0), axis=2
    )
    affinity_grad = (route_grad - jnp.sum(route_grad * shares, axis=-1, keepdims=True)) / totals
    return (
        affinity_grad,
        hidden_grad.reshape(saved_hidden.shape),
        down_grad.reshape(down_proj.shape),
    )


def solution(mesh):
    n_exp = mesh.shape["exp"]
    n_yh = 2
    n_rep = mesh.shape["rep"]
    split = Mesh(
        mesh.devices.reshape(n_rep // 2, 2, n_yh, n_exp // n_yh),
        ("rc", "core", "yh", "z"),
    )
    return jax.shard_map(
        on_device,
        mesh=split,
        in_specs=(
            P(TOKENS_SPEC, None),
            P(TOKENS_SPEC, None),
            P(TOKENS_SPEC, None),
            P(REP, ("yh", "z"), None, None, None),
            P(REP, ("yh", "z"), None),
        ),
        out_specs=(
            P(TOKENS_SPEC, None),
            P(REP, ("yh", "z"), None, None, None),
            P(REP, ("yh", "z"), None),
        ),
        check_vma=False,
    )
```

```python
import jax
import jax.numpy as jnp
from jax import lax
from jax.experimental import pallas as pl
from jax.experimental.pallas import tpu as pltpu
from jax.sharding import Mesh
from jax.sharding import PartitionSpec as P

ROUTE_SCALE = 2.5
TOKENS_SPEC = ("rc", "core", "yh", "z")
REP = ("rc", "core")
META = 128
MESH_ID = pl.DeviceIdType.MESH


def gather_weight_kernel(n, w_ref, out_ref, send_sem, recv_sem, fwd_send, fwd_recv, own_sem, local_sem):
    chip = lax.axis_index("rc")
    core = lax.axis_index("core")
    yh = lax.axis_index("yh")
    z = lax.axis_index("z")
    chips = n // 2
    me = chip * 2 + core
    partner = chip * 2 + (1 - core)
    barrier = pltpu.get_barrier_semaphore()
    for off in range(1, chips):
        peer = lax.rem(chip + off, chips) * 2 + core
        pl.semaphore_signal(barrier, inc=1, device_id=(peer // 2, peer % 2, yh, z), device_id_type=MESH_ID)
    pl.semaphore_signal(barrier, inc=1, device_id=(partner // 2, partner % 2, yh, z), device_id_type=MESH_ID)
    pl.semaphore_wait(barrier, chips)
    local = pltpu.make_async_copy(w_ref, out_ref.at[me], local_sem)
    local.start()
    own = pltpu.make_async_remote_copy(
        src_ref=w_ref,
        dst_ref=out_ref.at[me],
        send_sem=own_sem.at[0],
        recv_sem=own_sem.at[1],
        device_id=(partner // 2, partner % 2, yh, z),
        device_id_type=MESH_ID,
    )
    own.start()
    sends = []
    for off in range(1, chips):
        peer = lax.rem(chip + off, chips) * 2 + core
        copy = pltpu.make_async_remote_copy(
            src_ref=w_ref,
            dst_ref=out_ref.at[me],
            send_sem=send_sem.at[off],
            recv_sem=recv_sem.at[off],
            device_id=(peer // 2, peer % 2, yh, z),
            device_id_type=MESH_ID,
        )
        copy.start()
        sends.append(copy)
    forwards = []
    for off in range(1, chips):
        source = lax.rem(chip - off + chips, chips) * 2 + core
        incoming = pltpu.make_async_remote_copy(
            src_ref=w_ref,
            dst_ref=out_ref.at[source],
            send_sem=send_sem.at[off],
            recv_sem=recv_sem.at[off],
            device_id=(source // 2, source % 2, yh, z),
            device_id_type=MESH_ID,
        )
        incoming.wait_recv()
        forward = pltpu.make_async_remote_copy(
            src_ref=out_ref.at[source],
            dst_ref=out_ref.at[source],
            send_sem=fwd_send.at[off],
            recv_sem=fwd_recv.at[off],
            device_id=(partner // 2, partner % 2, yh, z),
            device_id_type=MESH_ID,
        )
        forward.start()
        forwards.append(forward)
    for copy in sends:
        copy.wait_send()
    own.wait_send()
    for forward in forwards:
        forward.wait_send()
    partner_own = pltpu.make_async_remote_copy(
        src_ref=w_ref,
        dst_ref=out_ref.at[partner],
        send_sem=own_sem.at[0],
        recv_sem=own_sem.at[1],
        device_id=(partner // 2, partner % 2, yh, z),
        device_id_type=MESH_ID,
    )
    partner_own.wait_recv()
    for off in range(1, chips):
        source = lax.rem(chip - off + chips, chips) * 2 + (1 - core)
        relayed = pltpu.make_async_remote_copy(
            src_ref=out_ref.at[source],
            dst_ref=out_ref.at[source],
            send_sem=fwd_send.at[off],
            recv_sem=fwd_recv.at[off],
            device_id=(partner // 2, partner % 2, yh, z),
            device_id_type=MESH_ID,
        )
        relayed.wait_recv()
    local.wait()


def gather_weight(w):
    n = lax.axis_size("rc") * lax.axis_size("core")
    rows, width = w.shape
    return pl.pallas_call(
        lambda *refs: gather_weight_kernel(n, *refs),
        out_shape=jax.ShapeDtypeStruct((n, rows, width), w.dtype),
        in_specs=[pl.BlockSpec(memory_space=pl.ANY)],
        out_specs=pl.BlockSpec(memory_space=pl.ANY),
        scratch_shapes=[
            pltpu.SemaphoreType.DMA((n // 2,)),
            pltpu.SemaphoreType.DMA((n // 2,)),
            pltpu.SemaphoreType.DMA((n // 2,)),
            pltpu.SemaphoreType.DMA((n // 2,)),
            pltpu.SemaphoreType.DMA((2,)),
            pltpu.SemaphoreType.DMA(()),
        ],
        compiler_params=pltpu.CompilerParams(collective_id=0, has_side_effects=True),
        cost_estimate=pl.CostEstimate(
            flops=0, transcendentals=0, bytes_accessed=2 * n * rows * width * w.dtype.itemsize
        ),
    )(w)


def partner_kernel(x_ref, out_ref, sems):
    chip = lax.axis_index("rc")
    core = lax.axis_index("core")
    yh = lax.axis_index("yh")
    z = lax.axis_index("z")
    other = 1 - core
    barrier = pltpu.get_barrier_semaphore()
    pl.semaphore_signal(barrier, inc=1, device_id=(chip, other, yh, z), device_id_type=MESH_ID)
    pl.semaphore_wait(barrier, 1)
    copy = pltpu.make_async_remote_copy(
        src_ref=x_ref.at[:, pl.ds(other, 1)],
        dst_ref=out_ref,
        send_sem=sems.at[0],
        recv_sem=sems.at[1],
        device_id=(chip, other, yh, z),
        device_id_type=MESH_ID,
    )
    copy.start()
    copy.wait()


def partner_rows(x):
    chips, cores, rows, width = x.shape
    return pl.pallas_call(
        partner_kernel,
        out_shape=jax.ShapeDtypeStruct((chips, 1, rows, width), x.dtype),
        in_specs=[pl.BlockSpec(memory_space=pl.ANY)],
        out_specs=pl.BlockSpec(memory_space=pl.ANY),
        scratch_shapes=[pltpu.SemaphoreType.DMA((2,))],
        compiler_params=pltpu.CompilerParams(collective_id=1, has_side_effects=True),
        cost_estimate=pl.CostEstimate(
            flops=0, transcendentals=0, bytes_accessed=chips * rows * width * x.dtype.itemsize
        ),
    )(x)


def local_slots(routes, expert_count):
    tok = routes.shape[0]
    expert_ids = jnp.arange(expert_count, dtype=jnp.int32)
    hits = routes[:, :, None] == expert_ids
    naming = jnp.sum(hits.astype(jnp.float32), axis=1)
    earlier = (
        jnp.arange(tok, dtype=jnp.int32)[None, :] < jnp.arange(tok, dtype=jnp.int32)[:, None]
    ).astype(jnp.bfloat16)
    before = jnp.dot(earlier, naming.astype(jnp.bfloat16), preferred_element_type=jnp.float32)
    return jnp.sum(jnp.where(hits, before[:, None, :], 0.0), axis=2)


def selection(route_f, slot_f, weight_f, expert, most):
    names = route_f == expert.astype(jnp.float32)
    position = jnp.sum(jnp.where(names, slot_f + 1.0, 0.0), axis=2) - 1.0
    weight = jnp.sum(jnp.where(names, weight_f, 0.0), axis=2)
    picks = position[:, None, :] == jnp.arange(most, dtype=jnp.float32)[None, :, None]
    packed_weight = jnp.sum(jnp.where(picks, weight[:, None, :], 0.0), axis=2)
    return picks.astype(jnp.bfloat16), packed_weight


def block_picks(picks):
    sources, most, tok = picks.shape
    eye = jnp.eye(sources, dtype=picks.dtype)
    return (picks[:, :, None, :] * eye[:, None, :, None]).reshape(sources * most, sources * tok)


def on_device(grad_out, routes, affinity, saved_hidden, down_proj):
    n_yh = lax.axis_size("yh")
    n_z = lax.axis_size("z")
    exp_devices = n_yh * n_z
    local_experts = down_proj.shape[1]
    expert_count = exp_devices * local_experts
    most = saved_hidden.shape[3]
    width = grad_out.shape[1]
    hidden_units = saved_hidden.shape[4]
    topk = routes.shape[1]
    tok = routes.shape[0]
    yh = lax.axis_index("yh")
    z = lax.axis_index("z")
    partner_yh = (yh + 1) % n_yh
    mine = yh * n_z + z
    partner = partner_yh * n_z + z

    totals = jnp.sum(affinity, axis=-1, keepdims=True)
    shares = affinity / totals
    route_weight = (ROUTE_SCALE * shares).astype(jnp.bfloat16)
    slots = local_slots(routes, expert_count)
    meta = jnp.concatenate(
        [
            routes.astype(jnp.bfloat16),
            slots.astype(jnp.bfloat16),
            route_weight,
            jnp.zeros((routes.shape[0], META - 3 * topk), jnp.bfloat16),
        ],
        axis=1,
    )
    half = width // 2
    swap = [(i, (i + 1) % n_yh) for i in range(n_yh)]
    first_part = jnp.concatenate([grad_out[:, :half], meta], axis=1)
    gathered_a = lax.all_gather(first_part, "z", axis=0, tiled=True)
    gathered_w = gather_weight(down_proj.reshape(-1, width)).reshape(hidden_units, width)
    gathered_a, gathered_w = lax.optimization_barrier((gathered_a, gathered_w))
    saved_hidden, gathered_w = lax.optimization_barrier((saved_hidden, gathered_w))
    meta_all = gathered_a[:, half : half + 3 * topk].astype(jnp.float32).reshape(n_z, tok, 3 * topk)
    route_f = meta_all[:, :, 0:topk]
    slot_f = meta_all[:, :, topk : 2 * topk]
    weight_f = meta_all[:, :, 2 * topk : 3 * topk]

    pick_mine, weight_mine = selection(route_f, slot_f, weight_f, mine, most)
    pick_partner, weight_partner = selection(route_f, slot_f, weight_f, partner, most)
    pick_mine = block_picks(pick_mine)
    pick_partner = block_picks(pick_partner)
    weight_far = lax.ppermute(weight_partner, "yh", perm=swap)

    def pack(gathered):
        out = jnp.dot(pick_partner, gathered, preferred_element_type=jnp.float32)
        far = lax.ppermute(out.astype(jnp.bfloat16), "yh", perm=swap)
        near = jnp.dot(pick_mine, gathered, preferred_element_type=jnp.float32)
        return near.astype(jnp.bfloat16), far

    near_a, far_a = pack(gathered_a[:, :half])
    gathered_b = lax.all_gather(grad_out[:, half:], "z", axis=0, tiled=True)
    near_b, far_b = pack(gathered_b)
    near_rows = jnp.concatenate([near_a, near_b], axis=1)
    far_rows = jnp.concatenate([far_a, far_b], axis=1)

    hidden = saved_hidden.reshape(exp_devices, most, hidden_units)
    plane = lambda x, p: lax.dynamic_slice_in_dim(x, p * n_z, n_z, axis=0)
    near_hidden = plane(hidden, yh).reshape(n_z * most, hidden_units)
    far_hidden = plane(hidden, partner_yh).reshape(n_z * most, hidden_units)

    def expert_side(rows, row_weight, hid):
        rows = rows.reshape(n_z * most, width)
        scale = row_weight.reshape(n_z * most, 1)
        projected = jnp.einsum(
            "rd,hd->rh", rows, gathered_w, preferred_element_type=jnp.float32
        )
        hidden_grad = (scale * projected).astype(jnp.bfloat16)
        combine = ROUTE_SCALE * jnp.sum(hid.astype(jnp.float32) * projected, axis=-1)
        scaled = (scale * rows.astype(jnp.float32)).astype(jnp.bfloat16)
        term = jnp.einsum("rh,rd->hd", hid, scaled, preferred_element_type=jnp.float32)
        return hidden_grad, combine, term

    near_grad, near_combine, near_term = expert_side(near_rows, weight_mine, near_hidden)
    far_grad, far_combine, far_term = expert_side(far_rows, weight_far, far_hidden)
    grad_term = near_term + far_term
    n_rc = lax.axis_size("rc")
    n_core = lax.axis_size("core")
    by_chip = grad_term.astype(jnp.bfloat16).reshape(n_rc, n_core, -1, width)
    received = partner_rows(by_chip)
    own = lax.dynamic_slice_in_dim(by_chip, lax.axis_index("core"), 1, axis=1)
    on_chip = (own.astype(jnp.float32) + received.astype(jnp.float32)).astype(jnp.bfloat16)
    down_grad = lax.psum_scatter(
        on_chip.reshape(n_rc, -1, width), "rc", scatter_dimension=0, tiled=True
    ).astype(jnp.float32)

    first = yh == 0
    hidden_grad = jnp.where(
        first,
        jnp.concatenate([near_grad, far_grad], axis=0),
        jnp.concatenate([far_grad, near_grad], axis=0),
    )
    combine_grad = jnp.where(
        first,
        jnp.concatenate([near_combine, far_combine], axis=0),
        jnp.concatenate([far_combine, near_combine], axis=0),
    ).reshape(exp_devices, most)
    returned = lax.all_to_all(
        combine_grad, ("yh", "z"), split_axis=0, concat_axis=0, tiled=True
    )
    expert_ids = jnp.arange(expert_count, dtype=jnp.int32)
    slot_ids = jnp.arange(most, dtype=jnp.float32)
    by_expert = jnp.sum(
        jnp.where((routes[:, :, None] == expert_ids)[:, :, :, None], returned[None, None], 0.0),
        axis=2,
    )
    route_grad = jnp.sum(
        jnp.where(slots[:, :, None] == slot_ids, by_expert, 0.0), axis=2
    )
    affinity_grad = (route_grad - jnp.sum(route_grad * shares, axis=-1, keepdims=True)) / totals
    return (
        affinity_grad,
        hidden_grad.reshape(saved_hidden.shape),
        down_grad.reshape(down_proj.shape),
    )


def solution(mesh):
    n_exp = mesh.shape["exp"]
    n_yh = 2
    n_rep = mesh.shape["rep"]
    split = Mesh(
        mesh.devices.reshape(n_rep // 2, 2, n_yh, n_exp // n_yh),
        ("rc", "core", "yh", "z"),
    )
    return jax.shard_map(
        on_device,
        mesh=split,
        in_specs=(
            P(TOKENS_SPEC, None),
            P(TOKENS_SPEC, None),
            P(TOKENS_SPEC, None),
            P(REP, ("yh", "z"), None, None, None),
            P(REP, ("yh", "z"), None),
        ),
        out_specs=(
            P(TOKENS_SPEC, None),
            P(REP, ("yh", "z"), None, None, None),
            P(REP, ("yh", "z"), None),
        ),
        check_vma=False,
    )
```
